32 devices in a mesh: ep: 8 (over z, x), rep: 4 (over y, core).
Axes of the slice: x: 2, y: 2, z: 4, core: 2. Of those that a mesh axis runs over, the one named last changes fastest.
Arguments:
- context: bfloat16 [2048, 2048], P(('ep', 'rep')), may hold values from -6 to 6
- residual: bfloat16 [2048, 2048], P(('ep', 'rep')), may hold values from -125 to 125
- out_proj: bfloat16 [2048, 2048], replicated, may hold values from -0.125 to 0.125
- attn_gain: bfloat16 [2048], replicated, may hold values from 0.25 to 1.75
- router: bfloat16 [2048, 64], replicated, may hold values from -18 to 18
- expert_ids: int32 [2048, 8], P(('ep', 'rep')), may hold values from 0 to 63, as said below
- gate_weight: bfloat16 [64, 2048, 1024], P('ep', None, 'rep'), may hold values from -0.125 to 0.125
- up_weight: bfloat16 [64, 2048, 1024], P('ep', None, 'rep'), may hold values from -0.125 to 0.125
- down_weight: bfloat16 [64, 2048, 1024], P('ep', None, 'rep'), may hold values from -1.5 to 1.5
- final_gain: bfloat16 [2048], replicated, may hold values from 0.25 to 1.75
Outputs:
- layer_out: bfloat16 [2048, 2048], P(('ep', 'rep'))
The draws below stay inside these ranges and needn't reach their ends.
Inputs may be any that keep to these rules, and one draw needn't show every extreme that they name: `expert_ids`: the rows of one device name exactly 32 distinct experts, each of them exactly 16 times. The entries of a row are distinct. Every expert is named by some row.
All inputs are finite; a program needn't handle non-finite values.
Results may differ from the reference program's by a relative error of at most 0.005.
Values may be sent and summed in bfloat16 or wider, within the bound.
A program may use at most 192 MiB of HBM per device.

```python
import jax
import jax.numpy as jnp
from jax import lax

D = 2048
FF = 1024
EXPERTS = 64
TOP = 8
ROW_DEV = 64
ROWS = 2048
CAP = 16
FQ = 256
N_EP = 8
N_REP = 4


def draw_router(key, part):
    router_draw = 0.6 * jnp.clip(jax.random.normal(jax.random.fold_in(key, 12), (D, EXPERTS), jnp.float32), -4.0, 4.0) * D ** (-0.5)
    return router_draw.astype(jnp.bfloat16)


def draw_residual(key, part):
    drawn_draw = jnp.clip(jax.random.normal(jax.random.fold_in(key, 21), (ROWS, D), jnp.float32), -4.0, 4.0)
    values = 0.7 * drawn_draw
    return values.astype(jnp.bfloat16)


def draw_expert_ids(key, part):
    device_total = ROWS // ROW_DEV
    circle = 4 * TOP
    ranking = jax.random.permutation(jax.random.fold_in(key, 31), EXPERTS).astype(jnp.int32)
    expert_range = jnp.arange(EXPERTS, dtype=jnp.int32)
    popular_rank = jnp.zeros((EXPERTS,), jnp.int32).at[ranking].set(expert_range)
    favour = jnp.where(popular_rank < EXPERTS // 8, 4096, jnp.where(popular_rank < 3 * EXPERTS // 8, 2048, 0)).astype(jnp.int32)

    def slot_permutation(slot_key):
        return jax.random.permutation(slot_key, TOP).astype(jnp.int32)

    def one_device(device_index):
        device_key = jax.random.fold_in(jax.random.fold_in(key, 32), device_index)
        jitter = jax.random.randint(jax.random.fold_in(device_key, 1), (EXPERTS,), 0, 4096, dtype=jnp.int32)
        first_forced = 2 * device_index % EXPERTS
        second_forced = (2 * device_index + 1) % EXPERTS
        forced = ((expert_range == first_forced) | (expert_range == second_forced)).astype(jnp.int32) * 65536
        scores = (jitter + favour + forced) * EXPERTS + expert_range
        _, chosen = lax.top_k(scores, circle)
        chosen = chosen.astype(jnp.int32)
        chosen = chosen[jax.random.permutation(jax.random.fold_in(device_key, 2), circle).astype(jnp.int32)]
        shifts = jax.random.randint(jax.random.fold_in(device_key, 3), (ROW_DEV // 4,), 0, circle, dtype=jnp.int32)
        row_number = jnp.arange(ROW_DEV, dtype=jnp.int32)
        starts = TOP * (row_number % 4) + shifts[row_number // 4]
        slot_order = jax.vmap(slot_permutation)(jax.random.split(jax.random.fold_in(device_key, 4), ROW_DEV))
        positions = (starts[:, None] + slot_order) % circle
        picked = chosen[positions]
        row_order = jax.random.permutation(jax.random.fold_in(device_key, 5), ROW_DEV).astype(jnp.int32)
        return picked[row_order]
    stacked = jax.vmap(one_device)(jnp.arange(device_total, dtype=jnp.int32))
    return stacked.reshape(ROWS, TOP).astype(jnp.int32)


def block_levels(key, dims, cuts, low, largest):
    gain, own = 1.0, jax.random.fold_in(key, 6)
    for position, blocks in cuts:
        draws = jnp.exp(jax.random.uniform(jax.random.fold_in(own, position), (blocks,), jnp.float32, low / len(cuts), largest / len(cuts)))
        gain = gain * jnp.repeat(draws, dims[position] // blocks).reshape([-1 if axis == position else 1 for axis in range(len(dims))])
    return gain


def normal_values(rng, shape, deviation, reach, shards=(), held_as=jnp.bfloat16):
    gain = block_levels(rng, shape, shards, -0.22, 0.18) if shards else 1.0
    values = jax.random.normal(rng, shape, jnp.float32) * deviation * gain
    return jnp.minimum(jnp.maximum(values, -reach), reach).astype(held_as)


def setup_inputs(seed: int = 0) -> dict:
    keys = jax.random.split(jax.random.key(seed), 11)
    return {
        "context": normal_values(keys[0], (ROWS, D), 1.0, 6.0, ((0, 32),)),
        "residual": draw_residual(jax.random.fold_in(keys[10], 71), 0),
        "out_proj": normal_values(keys[2], (D, D), D ** -0.5, 0.125),
        "attn_gain": jnp.clip(1.0 + 0.15 * jax.random.normal(keys[3], (D,), jnp.float32), 0.25, 1.75).astype(jnp.bfloat16),
        "router": draw_router(jax.random.fold_in(keys[10], 71), 0),
        "expert_ids": draw_expert_ids(jax.random.fold_in(keys[10], 71), 0),
        "gate_weight": normal_values(keys[6], (EXPERTS, D, FF), D ** -0.5, 0.125, ((0, 8), (2, 4))),
        "up_weight": normal_values(keys[7], (EXPERTS, D, FF), D ** -0.5, 0.125, ((0, 8), (2, 4))),
        "down_weight": normal_values(keys[8], (EXPERTS, D, FF), (max(FF // 64, 1)) ** -0.5, 1.5, ((0, 8), (2, 4))),
        "final_gain": jnp.clip(1.0 + 0.15 * jax.random.normal(keys[9], (D,), jnp.float32), 0.25, 1.75).astype(jnp.bfloat16),
    }


epsilon = 1e-05

def rms_scale(values, gain_vector):
    mean_square = lax.optimization_barrier(jnp.mean(values * values, axis=-1, keepdims=True))
    return values * lax.rsqrt(mean_square + epsilon) * gain_vector.astype(jnp.float32)

def reference(context, residual, out_proj, attn_gain, router, expert_ids, gate_weight, up_weight, down_weight, final_gain):
    devices = N_EP * N_REP
    pair_count = ROW_DEV * TOP
    attention = jnp.dot(context, out_proj, preferred_element_type=jnp.float32)
    mixed_stream = residual.astype(jnp.float32) + attention
    normed = rms_scale(mixed_stream, attn_gain).astype(jnp.bfloat16)
    logits = jnp.dot(normed, router, preferred_element_type=jnp.float32)
    probs = jax.nn.softmax(logits, axis=1)
    route_weight = jnp.take_along_axis(probs, expert_ids, axis=1)
    flat_ids = expert_ids.reshape(devices, pair_count)
    one_hot = (flat_ids[:, :, None] == jnp.arange(EXPERTS, dtype=jnp.int32)[None, None, :]).astype(jnp.int32)
    slot_rank = lax.optimization_barrier(jnp.sum(jnp.cumsum(one_hot, axis=1) * one_hot, axis=2)) - 1
    device_of = jnp.broadcast_to(jnp.arange(devices, dtype=jnp.int32)[:, None], (devices, pair_count))
    row_of = device_of * ROW_DEV + (jnp.arange(pair_count, dtype=jnp.int32) // TOP)[None, :]
    table = jnp.full((EXPERTS, devices, CAP), ROWS, jnp.int32).at[flat_ids, device_of, slot_rank].set(row_of)
    weight_table = jnp.zeros((EXPERTS, devices, CAP), jnp.float32).at[flat_ids, device_of, slot_rank].set(route_weight.reshape(devices, pair_count))
    padded = jnp.concatenate([normed, jnp.zeros((1, D), jnp.bfloat16)], axis=0)

    def one_expert(running, expert_index):
        row_index = table[expert_index].reshape(-1)
        batch_rows = padded[row_index]
        gate_all = gate_weight[expert_index]
        up_all = up_weight[expert_index]
        down_all = down_weight[expert_index]
        result = jnp.zeros((devices * CAP, D), jnp.float32)
        for quarter in range(N_REP):
            offset = quarter * FQ
            gate_proj = jnp.dot(batch_rows, gate_all[:, offset:offset + FQ], preferred_element_type=jnp.float32)
            up_proj = jnp.dot(batch_rows, up_all[:, offset:offset + FQ], preferred_element_type=jnp.float32)
            active = (jax.nn.silu(gate_proj) * up_proj).astype(jnp.bfloat16)
            part_sum = jnp.dot(active, down_all[:, offset:offset + FQ].T, preferred_element_type=jnp.float32)
            result = result + lax.optimization_barrier(part_sum.astype(jnp.bfloat16)).astype(jnp.float32)
        rounded = lax.optimization_barrier(result.astype(jnp.bfloat16)).astype(jnp.float32)
        contrib = weight_table[expert_index].reshape(-1, 1) * rounded
        return (running.at[row_index].add(contrib), None)
    start_sum = jnp.zeros((ROWS + 1, D), jnp.float32)
    expert_mix, _ = lax.scan(one_expert, start_sum, jnp.arange(EXPERTS, dtype=jnp.int32))
    total = mixed_stream + expert_mix[:ROWS]
    return rms_scale(total, final_gain).astype(jnp.bfloat16)
```

```python
import jax
import jax.numpy as jnp
from jax import lax
from jax.experimental import pallas as pl
from jax.experimental.pallas import tpu as pltpu
from jax.sharding import PartitionSpec as P

epsilon = 1e-05
capacity = 16


def rms_scale(values, gain_vector):
    mean_square = jnp.mean(values * values, axis=-1, keepdims=True)
    return values * lax.rsqrt(mean_square + epsilon) * gain_vector.astype(jnp.float32)


def front(context, residual, out_proj, attn_gain, router, expert_ids):
    expert_count = router.shape[1]
    attention = jnp.dot(context, out_proj, preferred_element_type=jnp.float32)
    mixed_stream = residual.astype(jnp.float32) + attention
    normed = rms_scale(mixed_stream, attn_gain).astype(jnp.bfloat16)
    logits = jnp.dot(normed, router, preferred_element_type=jnp.float32)
    probs = jax.nn.softmax(logits, axis=1)
    chosen = jnp.any(
        expert_ids[:, :, None] == jnp.arange(expert_count, dtype=jnp.int32)[None, None, :], axis=1
    )
    weights = jnp.where(chosen, probs, 0.0)
    return mixed_stream, normed, weights


def gathered(
    context, residual, out_proj, attn_gain, router, expert_ids,
    gate_weight, up_weight, down_weight, final_gain,
):
    row_count, model_width = context.shape
    local_experts = gate_weight.shape[0]
    owners = lax.axis_size("ep")
    sources = owners * lax.axis_size("rep")
    mixed_stream, normed, weights = front(
        context, residual, out_proj, attn_gain, router, expert_ids
    )
    high = weights.astype(jnp.bfloat16)
    low = (weights - high.astype(jnp.float32)).astype(jnp.bfloat16)
    block = jnp.concatenate([normed, high, low], axis=1)
    everyone = lax.all_gather(block, ("ep", "rep"), axis=0, tiled=False)
    rows = everyone[:, :, :model_width]
    first = model_width + lax.axis_index("ep") * local_experts
    high = lax.dynamic_slice_in_dim(everyone, first, local_experts, axis=2)
    low = lax.dynamic_slice_in_dim(everyone, first + weights.shape[1], local_experts, axis=2)
    local_weights = high.astype(jnp.float32) + low.astype(jnp.float32)
    mask = (local_weights > 0).astype(jnp.float32)
    earlier = (
        jnp.arange(row_count)[:, None] > jnp.arange(row_count)[None, :]
    ).astype(jnp.float32)
    rank = jnp.einsum("ij,sje->sie", earlier, mask)
    slots = jnp.arange(capacity, dtype=jnp.float32)
    placing = jnp.where(
        (rank[:, :, :, None] == slots) & (mask[:, :, :, None] > 0), 1.0, 0.0
    )
    slot_weight = jnp.sum(placing * local_weights[:, :, :, None], axis=1)
    placing = placing.astype(jnp.bfloat16).reshape(sources, row_count, local_experts * capacity)
    grouped = jnp.einsum(
        "sit,sid->std", placing, rows, preferred_element_type=jnp.float32
    ).astype(jnp.bfloat16)
    grouped = grouped.reshape(sources, local_experts, capacity, model_width)
    gate_proj = jnp.einsum(
        "serd,edw->serw", grouped, gate_weight, preferred_element_type=jnp.float32
    )
    up_proj = jnp.einsum("serd,edw->serw", grouped, up_weight, preferred_element_type=jnp.float32)
    active = (jax.nn.silu(gate_proj) * up_proj * slot_weight[..., None]).astype(jnp.bfloat16)
    part = jnp.einsum(
        "serw,edw->serd", active, down_weight, preferred_element_type=jnp.float32
    ).astype(jnp.bfloat16)
    part = part.reshape(sources, local_experts * capacity, model_width)
    share = jnp.einsum("sit,std->sid", placing, part, preferred_element_type=jnp.float32)
    share = share.astype(jnp.bfloat16).reshape(sources * row_count, model_width)
    expert_mix = lax.psum_scatter(share, ("ep", "rep"), scatter_dimension=0, tiled=True)
    total = mixed_stream + expert_mix.astype(jnp.float32)
    return rms_scale(total, final_gain).astype(jnp.bfloat16)


MESH = pl.DeviceIdType.MESH
LINE = 4
OWN, FLIP_X, FLIP_Y, FLIP_BOTH = 0, 1, 2, 3
ACROSS = 256
COUNTS = (
    ("line", LINE), ("x_low", LINE), ("x_high", LINE), ("y_low", LINE), ("y_high", LINE),
    ("far_low", LINE), ("far_high", LINE), ("pass", 4), ("plane", 4), ("plane_line", LINE),
    ("share", 4), ("y_first", LINE), ("x_first", LINE), ("x_next", LINE), ("y_next", LINE),
    ("x_last", LINE), ("y_last", LINE), ("line_end", LINE), ("back_line", LINE), ("back_plane", 4),
)
BASE = {name: sum(count for _, count in COUNTS[:i]) for i, (name, _) in enumerate(COUNTS)}
STRIDE = sum(count for _, count in COUNTS)
COPIES = 2 * STRIDE + 2


def wave_kernel(
    block_ref, mixed_ref, gain_ref, gate_hbm, up_hbm, down_hbm, out_ref,
    rows, gate, up, down, grouped, hits, weighted,
    comb, sib, first, follow, final, line_sum, back_line, back_plane, done, got,
    weight_sem, send_sem, recv_sem,
):
    half = block_ref.shape[0] // 2
    quarter = half // 2
    width = mixed_ref.shape[1]
    extra = block_ref.shape[1] - width
    local = gate.shape[0]
    chunk = 2 * LINE * half
    slots = LINE * capacity
    tile = 512
    tiles = width // tile

    ep, rep = lax.axis_index("ep"), lax.axis_index("rep")
    z, x, y, core = ep // 2, ep % 2, rep // 2, rep % 2
    across_x = (z * 2 + (1 - x), rep)
    across_y = (ep, (1 - y) * 2 + core)
    diagonal = (z * 2 + (1 - x), (1 - y) * 2 + core)
    sibling = (ep, y * 2 + (1 - core))
    planes = {FLIP_X: across_x, FLIP_Y: across_y, FLIP_BOTH: diagonal}

    def along_z(step):
        return (((z + step) % LINE) * 2 + x, rep)

    peers = [across_x, across_y, diagonal, sibling] + [along_z(step) for step in (1, 2, 3)]
    barrier = pltpu.get_barrier_semaphore()
    for peer in peers:
        pl.semaphore_signal(barrier, inc=1, device_id=peer, device_id_type=MESH)
    weight_copies = [
        pltpu.make_async_copy(source, target, weight_sem.at[i])
        for i, (source, target) in enumerate(((gate_hbm, gate), (up_hbm, up), (down_hbm, down)))
    ]
    for copy in weight_copies:
        copy.start()

    narrow = pl.ds(0, ACROSS)
    wide = pl.ds(ACROSS, width + extra - ACROSS)
    body = pl.ds(ACROSS, width - ACROSS)
    low, high = pl.ds(0, quarter), pl.ds(quarter, quarter)

    def remote(index, source, target, device):
        return pltpu.make_async_remote_copy(
            src_ref=source, dst_ref=target, send_sem=send_sem.at[index],
            recv_sem=recv_sem.at[index], device_id=device, device_id_type=MESH,
        )

    def copy_of(name, w, k):
        index = w * STRIDE + BASE[name] + k
        if name == "line":
            pair = rows.at[w, OWN, 0, core, :, wide], rows.at[w, OWN, k, core, :, wide], along_z(k)
        elif name in ("x_low", "x_high"):
            part = low if name == "x_low" else high
            pair = (
                rows.at[w, OWN, k, core, part, wide], rows.at[w, FLIP_X, k, core, part, wide],
                across_x,
            )
        elif name in ("y_low", "y_high"):
            part = low if name == "y_low" else high
            pair = (
                rows.at[w, OWN, k, core, part, wide], rows.at[w, FLIP_Y, k, core, part, wide],
                across_y,
            )
        elif name == "far_low":
            pair = (
                rows.at[w, FLIP_X, k, core, low, wide], rows.at[w, FLIP_BOTH, k, core, low, wide],
                across_y,
            )
        elif name == "far_high":
            pair = (
                rows.at[w, FLIP_Y, k, core, high, wide],
                rows.at[w, FLIP_BOTH, k, core, high, wide], across_x,
            )
        elif name == "pass":
            some = pl.ds(1, LINE - 1) if k == OWN else pl.ds(0, LINE)
            pair = rows.at[w, k, some, core], rows.at[w, k, some, core], sibling
        elif name == "plane":
            pair = (
                rows.at[w, OWN, 0, core, :, narrow], rows.at[w, k, 0, core, :, narrow], planes[k]
            )
        elif name == "plane_line":
            pair = (
                rows.at[w, :, 0, core, :, narrow], rows.at[w, :, k, core, :, narrow], along_z(k)
            )
        elif name == "share":
            pair = comb.at[w, k, 1 - core], sib.at[w, k], sibling
        elif name == "y_first":
            pair = comb.at[w, FLIP_BOTH, core, k, low, body], first.at[w, 0, k], across_y
        elif name == "x_first":
            pair = comb.at[w, FLIP_BOTH, core, k, high, body], first.at[w, 1, k], across_x
        elif name == "x_next":
            pair = comb.at[w, FLIP_X, core, k, high, body], follow.at[w, 1, k], across_x
        elif name == "y_next":
            pair = comb.at[w, FLIP_Y, core, k, low, body], follow.at[w, 0, k], across_y
        elif name == "x_last":
            pair = comb.at[w, FLIP_X, core, k, low, body], final.at[w, 0, k], across_x
        elif name == "y_last":
            pair = comb.at[w, FLIP_Y, core, k, high, body], final.at[w, 1, k], across_y
        elif name == "line_end":
            pair = comb.at[w, OWN, core, k, :, body], line_sum.at[w, k - 1], along_z(LINE - k)
        elif name == "back_line":
            pair = comb.at[w, :, core, k, :, narrow], back_line.at[w, k - 1], along_z(LINE - k)
        elif name == "back_plane":
            pair = comb.at[w, k, core, 0, :, narrow], back_plane.at[w, k - 1], planes[k]
        return remote(index, *pair)

    def start(name, w, k):
        copy_of(name, w, k).start()

    def arrive(name, w, k):
        copy_of(name, w, k).wait_recv()

    def begin_line(w):
        for k in (FLIP_X, FLIP_Y, FLIP_BOTH):
            start("plane", w, k)
        for k in (1, 3, 2):
            start("line", w, k)

    def spread(w, k):
        for name in ("x_low", "y_high", "y_low", "x_high"):
            start(name, w, k)

    def spread_next(w, k):
        arrive("line", w, k)
        spread(w, k)

    def plane_next(w):
        for k in (FLIP_X, FLIP_Y, FLIP_BOTH):
            arrive("plane", w, k)
        for k in (1, 3, 2):
            start("plane_line", w, k)

    def forward(w, k):
        arrive("x_low", w, k)
        start("far_low", w, k)
        arrive("y_high", w, k)
        start("far_high", w, k)

    def pass_own(w):
        for k in (1, 3, 2):
            arrive("plane_line", w, k)
        start("pass", w, OWN)

    def pass_x(w):
        for k in range(LINE):
            arrive("x_high", w, k)
        start("pass", w, FLIP_X)

    def pass_y(w):
        for k in range(LINE):
            arrive("y_low", w, k)
        start("pass", w, FLIP_Y)

    def pass_both(w):
        for k in range(LINE):
            arrive("far_low", w, k)
            arrive("far_high", w, k)
        start("pass", w, FLIP_BOTH)

    column_of = lax.broadcasted_iota(jnp.int32, (16, extra), 1)
    wanted = lax.broadcasted_iota(jnp.int32, (16, extra), 0)
    pick = jnp.where((column_of == ep * local + wanted) & (wanted < local), 1.0, 0.0).astype(
        jnp.bfloat16
    )
    above = lax.broadcasted_iota(jnp.int32, (chunk, chunk), 0)
    below = lax.broadcasted_iota(jnp.int32, (chunk, chunk), 1)
    earlier = jnp.where(
        (above < below) & (above // (2 * half) == below // (2 * half)), 1.0, 0.0
    ).astype(jnp.bfloat16)
    start_slot = (
        (lax.broadcasted_iota(jnp.int32, (16, chunk), 1) // (2 * half)) * capacity
    ).astype(jnp.float32)
    slot_number = lax.broadcasted_iota(jnp.int32, (slots, chunk), 0).astype(jnp.float32)

    def gather(w, place):
        arrive("pass", w, place)
        packed = rows[w, place, :, :, :, width:].reshape(chunk, extra)
        weight = lax.dot_general(
            pick, packed, (((1,), (1,)), ((), ())), preferred_element_type=jnp.float32
        )
        mask = jnp.where(weight > 0, 1.0, 0.0)
        rank = jnp.dot(mask.astype(jnp.bfloat16), earlier, preferred_element_type=jnp.float32)
        target = jnp.where(mask > 0, start_slot + rank, -1.0)
        for e in range(local):
            hit = target[e : e + 1, :] == slot_number
            hits[e] = jnp.where(hit, 1.0, 0.0).astype(jnp.bfloat16)
            weighted[place, e] = jnp.where(hit, weight[e : e + 1, :], 0.0).astype(jnp.bfloat16)
        table = hits[...].reshape(local * slots, chunk)

        @pl.loop(0, tiles)
        def _(t):
            span = pl.ds(pl.multiple_of(t * tile, tile), tile)
            piece = rows[w, place, :, :, :, span].reshape(chunk, tile)
            found = jnp.dot(table, piece, preferred_element_type=jnp.float32)
            grouped[:, place * slots : (place + 1) * slots, span] = found.astype(
                jnp.bfloat16
            ).reshape(local, slots, tile)

    def run_experts(beside):
        @pl.loop(0, local // 2)
        def _(i):
            beside(i)
            active = []
            for e in (2 * i, 2 * i + 1):
                batch = grouped[e]
                gate_proj = jnp.dot(batch, gate[e], preferred_element_type=jnp.float32)
                up_proj = jnp.dot(batch, up[e], preferred_element_type=jnp.float32)
                value = gate_proj / (1.0 + jnp.exp(-gate_proj)) * up_proj
                active.append(value.astype(jnp.bfloat16))
            for e, value in zip((2 * i, 2 * i + 1), active):
                for t in range(tiles):
                    part = lax.dot_general(
                        value, down[e, t * tile : (t + 1) * tile, :], (((1,), (1,)), ((), ())),
                        preferred_element_type=jnp.float32,
                    )
                    grouped[e, :, t * tile : (t + 1) * tile] = part.astype(jnp.bfloat16)

    def combine(w, place):
        table = weighted[place].reshape(local * slots, chunk)

        @pl.loop(0, tiles)
        def _(t):
            span = pl.ds(pl.multiple_of(t * tile, tile), tile)
            piece = grouped[:, place * slots : (place + 1) * slots, span]
            result = lax.dot_general(
                table, piece.reshape(local * slots, tile), (((0,), (0,)), ((), ())),
                preferred_element_type=jnp.float32,
            ).reshape(LINE, 2, half, tile).astype(jnp.bfloat16)
            for part in range(2):
                comb[w, place, part, :, :, span] = result[:, part]

        start("share", w, place)

    def add_into(target, *terms):
        total = target[...].astype(jnp.float32)
        for term in terms:
            total = total + term[...].astype(jnp.float32)
        target[...] = total.astype(jnp.bfloat16)

    def mine(w, place, k, part, span):
        return comb.at[w, place, core, k, part, span]

    def theirs(w, place, k, part, span):
        return sib.at[w, place, k, part, span]

    every = pl.ds(0, half)

    def send_both(w):
        arrive("share", w, FLIP_BOTH)
        for k in late:
            add_into(
                mine(w, FLIP_BOTH, k, every, body), theirs(w, FLIP_BOTH, k, every, body)
            )
            start("y_first", w, k)
            start("x_first", w, k)

    def send_x(w):
        arrive("share", w, FLIP_X)
        for k in late:
            add_into(mine(w, FLIP_X, k, high, body), theirs(w, FLIP_X, k, high, body))
            start("x_next", w, k)

    def send_y(w):
        arrive("share", w, FLIP_Y)
        for k in late:
            add_into(mine(w, FLIP_Y, k, low, body), theirs(w, FLIP_Y, k, low, body))
            start("y_next", w, k)

    def send_narrow(w):
        arrive("share", w, OWN)
        for k in late[:-1]:
            for place in range(4):
                add_into(mine(w, place, k, every, narrow), theirs(w, place, k, every, narrow))
            start("back_line", w, k)

    def turn(w, k):
        arrive("y_first", w, k)
        add_into(
            mine(w, FLIP_X, k, low, body), theirs(w, FLIP_X, k, low, body), first.at[w, 0, k]
        )
        start("x_last", w, k)
        arrive("x_first", w, k)
        add_into(
            mine(w, FLIP_Y, k, high, body), theirs(w, FLIP_Y, k, high, body), first.at[w, 1, k]
        )
        start("y_last", w, k)

    def turn_narrow(w):
        for k in late[:-1]:
            arrive("back_line", w, k)
        for place in (FLIP_BOTH, FLIP_X, FLIP_Y, OWN):
            add_into(
                mine(w, place, 0, every, narrow), theirs(w, place, 0, every, narrow),
                *(back_line.at[w, k, place] for k in range(LINE - 1)),
            )
            if place != OWN:
                start("back_plane", w, place)

    def finish(w, k):
        arrive("y_next", w, k)
        arrive("x_last", w, k)
        add_into(
            mine(w, OWN, k, low, body), theirs(w, OWN, k, low, body),
            follow.at[w, 0, k], final.at[w, 0, k],
        )
        arrive("x_next", w, k)
        arrive("y_last", w, k)
        add_into(
            mine(w, OWN, k, high, body), theirs(w, OWN, k, high, body),
            follow.at[w, 1, k], final.at[w, 1, k],
        )

    def conclude(w):
        for k in late[:-1]:
            arrive("line_end", w, k)
        for place in (FLIP_X, FLIP_Y, FLIP_BOTH):
            arrive("back_plane", w, place)
        total = comb[w, OWN, core, 0, :, body].astype(jnp.float32)
        for k in range(LINE - 1):
            total = total + line_sum[w, k].astype(jnp.float32)
        done[w, :, body] = total
        total = comb[w, OWN, core, 0, :, narrow].astype(jnp.float32)
        for k in range(3):
            total = total + back_plane[w, k].astype(jnp.float32)
        done[w, :, narrow] = total

    late = (2, 1, 3, 0)
    pl.semaphore_wait(barrier, len(peers))
    rows[core, OWN, 0, 0] = block_ref[:half]
    rows[core, OWN, 0, 1] = block_ref[half:]
    exchange = remote(2 * STRIDE, rows.at[core, OWN, 0], rows.at[core, OWN, 0], sibling)
    exchange.start()
    remote(2 * STRIDE, rows.at[1 - core, OWN, 0], rows.at[1 - core, OWN, 0], sibling).wait_recv()

    begin_line(0)
    spread(0, 0)
    plane_next(0)
    spread_next(0, 1)
    forward(0, 0)
    spread_next(0, 3)
    forward(0, 1)
    spread_next(0, 2)
    begin_line(1)
    pass_own(0)
    forward(0, 3)
    plane_next(1)
    gather(0, OWN)
    forward(0, 2)
    pass_x(0)
    pass_y(0)
    spread(1, 0)
    gather(0, FLIP_X)
    gather(0, FLIP_Y)
    pass_both(0)
    gather(0, FLIP_BOTH)
    for copy in weight_copies:
        copy.wait()

    def spread_beside(i):
        @pl.when(i < LINE - 1)
        def _():
            spread_next(1, i + 1)

    run_experts(spread_beside)
    combine(0, FLIP_BOTH)
    forward(1, 0)
    combine(0, FLIP_X)
    send_both(0)
    forward(1, 1)
    combine(0, FLIP_Y)
    send_x(0)
    forward(1, 2)
    combine(0, OWN)
    send_y(0)
    forward(1, 3)
    send_narrow(0)
    pass_own(1)
    pass_x(1)
    pass_y(1)
    gather(1, OWN)
    turn(0, late[0])
    turn(0, late[1])
    gather(1, FLIP_X)
    turn(0, late[2])
    turn(0, late[3])
    gather(1, FLIP_Y)
    pass_both(1)
    turn_narrow(0)
    gather(1, FLIP_BOTH)

    def finish_beside(i):
        k = LINE - 1 - i
        finish(0, k)

        @pl.when(k > 0)
        def _():
            start("line_end", 0, k)

    run_experts(finish_beside)
    combine(1, FLIP_BOTH)
    combine(1, FLIP_X)
    send_both(1)
    combine(1, FLIP_Y)
    send_x(1)
    combine(1, OWN)
    send_y(1)
    send_narrow(1)
    conclude(0)
    turn(1, late[0])
    turn(1, late[1])
    turn_narrow(1)
    for i, k in enumerate(late):
        finish(1, k)
        if k:
            start("line_end", 1, k)
        if i + 2 < LINE:
            turn(1, late[i + 2])
    conclude(1)
    hand_over = remote(2 * STRIDE + 1, done.at[1 - core], got, sibling)
    hand_over.start()
    gain = gain_ref[...].astype(jnp.float32)

    def finalize(total, part):
        span = pl.ds(pl.multiple_of(part * half, half), half)
        total = total + mixed_ref[span]
        mean_square = jnp.mean(total * total, axis=-1, keepdims=True)
        out_ref[span] = (total * lax.rsqrt(mean_square + epsilon) * gain).astype(jnp.bfloat16)

    finalize(done[core], core)
    hand_over.wait_recv()
    finalize(got[...], 1 - core)
    hand_over.wait_send()
    exchange.wait_send()
    skip = ("line", "plane", "plane_line", "line_end", "back_line", "back_plane")
    for w in range(2):
        for name, count in COUNTS:
            for k in range(1 if name in skip else 0, count):
                copy_of(name, w, k).wait_send()


def waves(
    context, residual, out_proj, attn_gain, router, expert_ids,
    gate_weight, up_weight, down_weight, final_gain,
):
    row_count, width = context.shape
    mixed_stream, normed, weights = front(
        context, residual, out_proj, attn_gain, router, expert_ids
    )
    top = weights.astype(jnp.bfloat16)
    block = jnp.concatenate([normed, top, jnp.zeros_like(top)], axis=1)
    half = row_count // 2
    quarter = half // 2
    local = gate_weight.shape[0]
    slots = LINE * capacity
    chunk = 2 * LINE * half
    rest = width - ACROSS
    low = jnp.bfloat16
    vmem = pl.BlockSpec(memory_space=pltpu.VMEM)
    hbm = pl.BlockSpec(memory_space=pl.ANY)
    return pl.pallas_call(
        wave_kernel,
        out_shape=jax.ShapeDtypeStruct((row_count, width), low),
        in_specs=[vmem, vmem, vmem, hbm, hbm, hbm],
        out_specs=vmem,
        scratch_shapes=[
            pltpu.VMEM((2, 4, LINE, 2, half, block.shape[1]), low),
            pltpu.VMEM(gate_weight.shape, low),
            pltpu.VMEM(up_weight.shape, low),
            pltpu.VMEM(down_weight.shape, low),
            pltpu.VMEM((local, 4 * slots, width), low),
            pltpu.VMEM((local, slots, chunk), low),
            pltpu.VMEM((4, local, slots, chunk), low),
            pltpu.VMEM((2, 4, 2, LINE, half, width), low),
            pltpu.VMEM((2, 4, LINE, half, width), low),
            pltpu.VMEM((2, 2, LINE, quarter, rest), low),
            pltpu.VMEM((2, 2, LINE, quarter, rest), low),
            pltpu.VMEM((2, 2, LINE, quarter, rest), low),
            pltpu.VMEM((2, LINE - 1, half, rest), low),
            pltpu.VMEM((2, LINE - 1, 4, half, ACROSS), low),
            pltpu.VMEM((2, 3, half, ACROSS), low),
            pltpu.VMEM((2, half, width), jnp.float32),
            pltpu.VMEM((half, width), jnp.float32),
            pltpu.SemaphoreType.DMA((3,)),
            pltpu.SemaphoreType.DMA((COPIES,)),
            pltpu.SemaphoreType.DMA((COPIES,)),
        ],
        compiler_params=pltpu.CompilerParams(
            collective_id=0, has_side_effects=True, vmem_limit_bytes=63 * 1024 * 1024
        ),
    )(block, mixed_stream, final_gain.reshape(1, width), gate_weight, up_weight, down_weight)


def solution(mesh):
    per_device = waves if dict(mesh.shape) == {"ep": 2 * LINE, "rep": 4} else gathered
    in_specs = (
        P(("ep", "rep"), None),
        P(("ep", "rep"), None),
        P(),
        P(),
        P(),
        P(("ep", "rep"), None),
        P("ep", None, "rep"),
        P("ep", None, "rep"),
        P("ep", None, "rep"),
        P(),
    )
    out_specs = P(("ep", "rep"), None)
    return jax.shard_map(
        per_device, mesh=mesh, in_specs=in_specs, out_specs=out_specs, check_vma=False
    )
```

```python
import jax
import jax.numpy as jnp
from jax import lax
from jax.experimental import pallas as pl
from jax.experimental.pallas import tpu as pltpu
from jax.sharding import PartitionSpec as P

epsilon = 1e-05
capacity = 16


def rms_scale(values, gain_vector):
    mean_square = jnp.mean(values * values, axis=-1, keepdims=True)
    return values * lax.rsqrt(mean_square + epsilon) * gain_vector.astype(jnp.float32)


def front(context, residual, out_proj, attn_gain, router, expert_ids):
    expert_count = router.shape[1]
    attention = jnp.dot(context, out_proj, preferred_element_type=jnp.float32)
    mixed_stream = residual.astype(jnp.float32) + attention
    normed = rms_scale(mixed_stream, attn_gain).astype(jnp.bfloat16)
    logits = jnp.dot(normed, router, preferred_element_type=jnp.float32)
    probs = jax.nn.softmax(logits, axis=1)
    chosen = jnp.any(
        expert_ids[:, :, None] == jnp.arange(expert_count, dtype=jnp.int32)[None, None, :], axis=1
    )
    weights = jnp.where(chosen, probs, 0.0)
    return mixed_stream, normed, weights


def gathered(
    context, residual, out_proj, attn_gain, router, expert_ids,
    gate_weight, up_weight, down_weight, final_gain,
):
    row_count, model_width = context.shape
    local_experts = gate_weight.shape[0]
    owners = lax.axis_size("ep")
    sources = owners * lax.axis_size("rep")
    mixed_stream, normed, weights = front(
        context, residual, out_proj, attn_gain, router, expert_ids
    )
    high = weights.astype(jnp.bfloat16)
    low = (weights - high.astype(jnp.float32)).astype(jnp.bfloat16)
    block = jnp.concatenate([normed, high, low], axis=1)
    everyone = lax.all_gather(block, ("ep", "rep"), axis=0, tiled=False)
    rows = everyone[:, :, :model_width]
    first = model_width + lax.axis_index("ep") * local_experts
    high = lax.dynamic_slice_in_dim(everyone, first, local_experts, axis=2)
    low = lax.dynamic_slice_in_dim(everyone, first + weights.shape[1], local_experts, axis=2)
    local_weights = high.astype(jnp.float32) + low.astype(jnp.float32)
    mask = (local_weights > 0).astype(jnp.float32)
    earlier = (
        jnp.arange(row_count)[:, None] > jnp.arange(row_count)[None, :]
    ).astype(jnp.float32)
    rank = jnp.einsum("ij,sje->sie", earlier, mask)
    slots = jnp.arange(capacity, dtype=jnp.float32)
    placing = jnp.where(
        (rank[:, :, :, None] == slots) & (mask[:, :, :, None] > 0), 1.0, 0.0
    )
    slot_weight = jnp.sum(placing * local_weights[:, :, :, None], axis=1)
    placing = placing.astype(jnp.bfloat16).reshape(sources, row_count, local_experts * capacity)
    grouped = jnp.einsum(
        "sit,sid->std", placing, rows, preferred_element_type=jnp.float32
    ).astype(jnp.bfloat16)
    grouped = grouped.reshape(sources, local_experts, capacity, model_width)
    gate_proj = jnp.einsum(
        "serd,edw->serw", grouped, gate_weight, preferred_element_type=jnp.float32
    )
    up_proj = jnp.einsum("serd,edw->serw", grouped, up_weight, preferred_element_type=jnp.float32)
    active = (jax.nn.silu(gate_proj) * up_proj * slot_weight[..., None]).astype(jnp.bfloat16)
    part = jnp.einsum(
        "serw,edw->serd", active, down_weight, preferred_element_type=jnp.float32
    ).astype(jnp.bfloat16)
    part = part.reshape(sources, local_experts * capacity, model_width)
    share = jnp.einsum("sit,std->sid", placing, part, preferred_element_type=jnp.float32)
    share = share.astype(jnp.bfloat16).reshape(sources * row_count, model_width)
    expert_mix = lax.psum_scatter(share, ("ep", "rep"), scatter_dimension=0, tiled=True)
    total = mixed_stream + expert_mix.astype(jnp.float32)
    return rms_scale(total, final_gain).astype(jnp.bfloat16)


MESH = pl.DeviceIdType.MESH
LINE = 4
OWN, FLIP_X, FLIP_Y, FLIP_BOTH = 0, 1, 2, 3
GO_ACROSS, BACK_ACROSS = 256, 256
COUNTS = (
    ("right", LINE), ("left", LINE), ("x_low", LINE), ("x_high", LINE), ("y_low", LINE),
    ("y_high", LINE), ("far_low", LINE), ("far_high", LINE), ("pass", 4), ("pass_narrow", 1),
    ("plane", 4), ("plane_right", LINE), ("plane_left", LINE),
    ("share", 4), ("y_first", LINE), ("x_first", LINE), ("x_next", LINE), ("y_next", LINE),
    ("x_last", LINE), ("y_last", LINE), ("line_end", LINE), ("back_line", LINE), ("back_plane", 4),
)
BASE = {name: sum(count for _, count in COUNTS[:i]) for i, (name, _) in enumerate(COUNTS)}
STRIDE = sum(count for _, count in COUNTS)
COPIES = 2 * STRIDE + 2


def wave_kernel(
    block_ref, mixed_ref, gain_ref, gate_hbm, up_hbm, down_hbm, out_ref,
    rows, gate, up, down, grouped, hits, weighted,
    comb, sib, first, follow, final, line_sum, back_line, back_plane, done, got,
    weight_sem, send_sem, recv_sem,
):
    half = block_ref.shape[0] // 2
    quarter = half // 2
    width = mixed_ref.shape[1]
    extra = block_ref.shape[1] - width
    local = gate.shape[0]
    chunk = 2 * LINE * half
    slots = LINE * capacity
    tile = 512

    ep, rep = lax.axis_index("ep"), lax.axis_index("rep")
    z, x, y, core = ep // 2, ep % 2, rep // 2, rep % 2
    across_x = (z * 2 + (1 - x), rep)
    across_y = (ep, (1 - y) * 2 + core)
    diagonal = (z * 2 + (1 - x), (1 - y) * 2 + core)
    sibling = (ep, y * 2 + (1 - core))
    planes = {FLIP_X: across_x, FLIP_Y: across_y, FLIP_BOTH: diagonal}

    def along_z(step):
        return (((z + step) % LINE) * 2 + x, rep)

    peers = [across_x, across_y, diagonal, sibling] + [along_z(step) for step in (1, 2, 3)]
    barrier = pltpu.get_barrier_semaphore()
    for peer in peers:
        pl.semaphore_signal(barrier, inc=1, device_id=peer, device_id_type=MESH)
    weight_copies = [
        pltpu.make_async_copy(source, target, weight_sem.at[i])
        for i, (source, target) in enumerate(((gate_hbm, gate), (up_hbm, up), (down_hbm, down)))
    ]
    for copy in weight_copies:
        copy.start()

    slim = pl.ds(0, GO_ACROSS)
    wide = pl.ds(GO_ACROSS, width + extra - GO_ACROSS)
    narrow = pl.ds(0, BACK_ACROSS)
    body = pl.ds(BACK_ACROSS, width - BACK_ACROSS)
    low, high = pl.ds(0, quarter), pl.ds(quarter, quarter)

    def remote(index, source, target, device):
        return pltpu.make_async_remote_copy(
            src_ref=source, dst_ref=target, send_sem=send_sem.at[index],
            recv_sem=recv_sem.at[index], device_id=device, device_id_type=MESH,
        )

    def column(k):
        return (z + k) % LINE

    tours = tuple(
        sum(place * LINE**i for i, place in enumerate(tour))
        for tour in ((0, 1, 2, 3), (1, 0, 2, 3), (2, 3, 1, 0), (3, 2, 1, 0))
    )
    tour = jnp.where(z < 2, jnp.where(z == 0, *tours[:2]), jnp.where(z == 2, *tours[2:]))

    def stop(n):
        power = 1
        for i in range(1, LINE):
            power = power * (1 + (LINE - 1) * jnp.where(n >= i, 1, 0))
        return (tour // power) % LINE

    def copy_of(name, w, k):
        index = w * STRIDE + BASE[name] + k
        if name == "right":
            at = rows.at[w, OWN, (z - k + LINE) % LINE, core, :, wide]
            pair = at, at, along_z(1)
        elif name == "left":
            at = rows.at[w, OWN, (z + k) % LINE, core, :, wide]
            pair = at, at, along_z(LINE - 1)
        elif name == "plane_right":
            at = rows.at[w, :, (z - k + LINE) % LINE, core, :, slim]
            pair = at, at, along_z(1)
        elif name == "plane_left":
            at = rows.at[w, :, (z + k) % LINE, core, :, slim]
            pair = at, at, along_z(LINE - 1)
        elif name in ("x_low", "x_high"):
            part = low if name == "x_low" else high
            pair = (
                rows.at[w, OWN, k, core, part, wide], rows.at[w, FLIP_X, k, core, part, wide],
                across_x,
            )
        elif name in ("y_low", "y_high"):
            part = low if name == "y_low" else high
            pair = (
                rows.at[w, OWN, k, core, part, wide], rows.at[w, FLIP_Y, k, core, part, wide],
                across_y,
            )
        elif name == "far_low":
            pair = (
                rows.at[w, FLIP_X, k, core, low, wide], rows.at[w, FLIP_BOTH, k, core, low, wide],
                across_y,
            )
        elif name == "far_high":
            pair = (
                rows.at[w, FLIP_Y, k, core, high, wide],
                rows.at[w, FLIP_BOTH, k, core, high, wide], across_x,
            )
        elif name == "pass":
            at = rows.at[w, k, :, core, :, wide]
            pair = at, at, sibling
        elif name == "pass_narrow":
            at = rows.at[w, :, :, core, :, slim]
            pair = at, at, sibling
        elif name == "plane":
            pair = rows.at[w, OWN, z, core, :, slim], rows.at[w, k, z, core, :, slim], planes[k]
        elif name == "share":
            pair = comb.at[w, k, 1 - core], sib.at[w, k], sibling
        elif name == "y_first":
            pair = comb.at[w, FLIP_BOTH, core, column(k), low, body], first.at[w, 0, k], across_y
        elif name == "x_first":
            pair = comb.at[w, FLIP_BOTH, core, column(k), high, body], first.at[w, 1, k], across_x
        elif name == "x_next":
            pair = comb.at[w, FLIP_X, core, column(k), high, body], follow.at[w, 1, k], across_x
        elif name == "y_next":
            pair = comb.at[w, FLIP_Y, core, column(k), low, body], follow.at[w, 0, k], across_y
        elif name == "x_last":
            pair = comb.at[w, FLIP_X, core, column(k), low, body], final.at[w, 0, k], across_x
        elif name == "y_last":
            pair = comb.at[w, FLIP_Y, core, column(k), high, body], final.at[w, 1, k], across_y
        elif name == "line_end":
            pair = (
                comb.at[w, OWN, core, column(k), :, body], line_sum.at[w, k - 1], along_z(k)
            )
        elif name == "back_line":
            pair = comb.at[w, :, core, column(k), :, narrow], back_line.at[w, k - 1], along_z(k)
        elif name == "back_plane":
            pair = comb.at[w, k, core, z, :, narrow], back_plane.at[w, k - 1], planes[k]
        return remote(index, *pair)

    def start(name, w, k):
        copy_of(name, w, k).start()

    def arrive(name, w, k):
        copy_of(name, w, k).wait_recv()

    def spread(w, k):
        for name in ("x_low", "y_high", "y_low", "x_high"):
            start(name, w, k)

    def start_line(w, right, left):
        pl.when(z < LINE - 1)(lambda: start(right, w, 0))
        pl.when(z > 0)(lambda: start(left, w, 0))

    def begin(w):
        for k in (FLIP_X, FLIP_Y, FLIP_BOTH):
            start("plane", w, k)
        start_line(w, "right", "left")

    def plane_next(w):
        for k in (FLIP_X, FLIP_Y, FLIP_BOTH):
            arrive("plane", w, k)
        start_line(w, "plane_right", "plane_left")

    def along(w, n, right, left, at):
        source = stop(n)
        index = w * STRIDE + jnp.where(
            source < z, BASE[right] + z - source - 1, BASE[left] + source - z - 1
        )
        remote(index, at(source), at(source), across_x).wait_recv()
        pl.when((source < z) & (z < LINE - 1))(lambda: start(right, w, z - source))
        pl.when((source > z) & (z > 0))(lambda: start(left, w, source - z))
        return source

    def line_next(w, n):
        spread(w, along(w, n, "right", "left", lambda k: rows.at[w, OWN, k, core, :, wide]))

    def narrow_next(w, n):
        along(w, n, "plane_right", "plane_left", lambda k: rows.at[w, :, k, core, :, slim])

    def forward(w, n):
        k = stop(n)
        arrive("x_low", w, k)
        start("far_low", w, k)
        arrive("y_high", w, k)
        start("far_high", w, k)

    def pass_x(w):
        for k in range(LINE):
            arrive("x_high", w, k)
        start("pass", w, FLIP_X)

    def pass_y(w):
        for k in range(LINE):
            arrive("y_low", w, k)
        start("pass", w, FLIP_Y)

    def pass_both(w):
        for k in range(LINE):
            arrive("far_low", w, k)
            arrive("far_high", w, k)
        start("pass", w, FLIP_BOTH)

    column_of = lax.broadcasted_iota(jnp.int32, (16, extra), 1)
    wanted = lax.broadcasted_iota(jnp.int32, (16, extra), 0)
    pick = jnp.where((column_of == ep * local + wanted) & (wanted < local), 1.0, 0.0).astype(
        jnp.bfloat16
    )
    above = lax.broadcasted_iota(jnp.int32, (chunk, chunk), 0)
    below = lax.broadcasted_iota(jnp.int32, (chunk, chunk), 1)
    earlier = jnp.where(
        (above < below) & (above // (2 * half) == below // (2 * half)), 1.0, 0.0
    ).astype(jnp.bfloat16)
    start_slot = (
        (lax.broadcasted_iota(jnp.int32, (16, chunk), 1) // (2 * half)) * capacity
    ).astype(jnp.float32)
    slot_number = lax.broadcasted_iota(jnp.int32, (slots, chunk), 0).astype(jnp.float32)

    def gather(w, place):
        arrive("pass", w, place)
        packed = rows[w, place, :, :, :, width:].reshape(chunk, extra)
        weight = lax.dot_general(
            pick, packed, (((1,), (1,)), ((), ())), preferred_element_type=jnp.float32
        )
        mask = jnp.where(weight > 0, 1.0, 0.0)
        rank = jnp.dot(mask.astype(jnp.bfloat16), earlier, preferred_element_type=jnp.float32)
        target = jnp.where(mask > 0, start_slot + rank, -1.0)
        for e in range(local):
            hit = target[e : e + 1, :] == slot_number
            hits[place, e] = jnp.where(hit, 1.0, 0.0).astype(jnp.bfloat16)
            weighted[place, e] = jnp.where(hit, weight[e : e + 1, :], 0.0).astype(jnp.bfloat16)
        fill(w, place, pl.ds(GO_ACROSS, width - GO_ACROSS))

    def fill(w, place, span):
        found = jnp.dot(
            hits[place].reshape(local * slots, chunk),
            rows[w, place, :, :, :, span].reshape(chunk, span.size),
            preferred_element_type=jnp.float32,
        )
        grouped[:, place * slots : (place + 1) * slots, span] = found.astype(
            jnp.bfloat16
        ).reshape(local, slots, span.size)

    def gather_narrow(w):
        arrive("pass_narrow", w, 0)
        for place in range(4):
            fill(w, place, slim)

    def run_experts(beside):
        @pl.loop(0, local // 2)
        def _(i):
            beside(i)
            active = []
            for e in (2 * i, 2 * i + 1):
                batch = grouped[e]
                gate_proj = jnp.dot(batch, gate[e], preferred_element_type=jnp.float32)
                up_proj = jnp.dot(batch, up[e], preferred_element_type=jnp.float32)
                value = gate_proj / (1.0 + jnp.exp(-gate_proj)) * up_proj
                active.append(value.astype(jnp.bfloat16))
            for e, value in zip((2 * i, 2 * i + 1), active):
                for t in range(width // tile):
                    part = lax.dot_general(
                        value, down[e, t * tile : (t + 1) * tile, :], (((1,), (1,)), ((), ())),
                        preferred_element_type=jnp.float32,
                    )
                    grouped[e, :, t * tile : (t + 1) * tile] = part.astype(jnp.bfloat16)

    def combine(w, place):
        table = weighted[place].reshape(local * slots, chunk)
        piece = grouped[:, place * slots : (place + 1) * slots, :].reshape(local * slots, width)
        result = lax.dot_general(
            table, piece, (((0,), (0,)), ((), ())), preferred_element_type=jnp.float32
        ).astype(jnp.bfloat16).reshape(LINE, 2, half, width)
        for part in range(2):
            comb[w, place, part] = result[:, part]
        start("share", w, place)

    def add_into(target, *terms):
        total = target[...].astype(jnp.float32)
        for term in terms:
            total = total + term[...].astype(jnp.float32)
        target[...] = total.astype(jnp.bfloat16)

    def mine(w, place, k, part, span):
        return comb.at[w, place, core, column(k), part, span]

    def theirs(w, place, k, part, span):
        return sib.at[w, place, column(k), part, span]

    every = pl.ds(0, half)

    def send_both(w):
        arrive("share", w, FLIP_BOTH)
        for k in late:
            add_into(
                mine(w, FLIP_BOTH, k, every, body), theirs(w, FLIP_BOTH, k, every, body)
            )
            start("y_first", w, k)
            start("x_first", w, k)

    def send_narrow(w):
        arrive("share", w, OWN)
        for k in late[:-1]:
            for place in range(4):
                add_into(mine(w, place, k, every, narrow), theirs(w, place, k, every, narrow))
            start("back_line", w, k)

    def turn(w, k):
        arrive("y_first", w, k)
        add_into(
            mine(w, FLIP_X, k, low, body), theirs(w, FLIP_X, k, low, body), first.at[w, 0, k]
        )
        start("x_last", w, k)
        arrive("x_first", w, k)
        add_into(
            mine(w, FLIP_Y, k, high, body), theirs(w, FLIP_Y, k, high, body), first.at[w, 1, k]
        )
        start("y_last", w, k)
        add_into(mine(w, FLIP_X, k, high, body), theirs(w, FLIP_X, k, high, body))
        start("x_next", w, k)
        add_into(mine(w, FLIP_Y, k, low, body), theirs(w, FLIP_Y, k, low, body))
        start("y_next", w, k)

    def turn_narrow(w):
        for k in late[:-1]:
            arrive("back_line", w, k)
        for place in (FLIP_BOTH, FLIP_X, FLIP_Y, OWN):
            add_into(
                mine(w, place, 0, every, narrow), theirs(w, place, 0, every, narrow),
                *(back_line.at[w, k, place] for k in range(LINE - 1)),
            )
            if place != OWN:
                start("back_plane", w, place)

    def finish(w, k):
        arrive("y_next", w, k)
        arrive("x_last", w, k)
        add_into(
            mine(w, OWN, k, low, body), theirs(w, OWN, k, low, body),
            follow.at[w, 0, k], final.at[w, 0, k],
        )
        arrive("x_next", w, k)
        arrive("y_last", w, k)
        add_into(
            mine(w, OWN, k, high, body), theirs(w, OWN, k, high, body),
            follow.at[w, 1, k], final.at[w, 1, k],
        )

    def conclude(w):
        for k in late[:-1]:
            arrive("line_end", w, k)
        for place in (FLIP_X, FLIP_Y, FLIP_BOTH):
            arrive("back_plane", w, place)
        total = comb[w, OWN, core, z, :, body].astype(jnp.float32)
        for k in range(LINE - 1):
            total = total + line_sum[w, k].astype(jnp.float32)
        done[w, :, body] = total
        total = comb[w, OWN, core, z, :, narrow].astype(jnp.float32)
        for k in range(3):
            total = total + back_plane[w, k].astype(jnp.float32)
        done[w, :, narrow] = total

    late = (2, 1, 3, 0)
    pl.semaphore_wait(barrier, len(peers))
    rows[core, OWN, z, core] = block_ref[pl.ds(pl.multiple_of(core * half, half), half)]
    given = block_ref.at[pl.ds(pl.multiple_of((1 - core) * half, half), half)]
    taken = rows.at[1 - core, OWN, z, core]
    exchange = remote(2 * STRIDE, given, rows.at[core, OWN, z, 1 - core], sibling)
    exchange.start()
    remote(2 * STRIDE, taken, taken, sibling).wait_recv()

    begin(0)
    spread(0, z)
    line_next(0, 1)
    plane_next(0)
    forward(0, 0)
    line_next(0, 2)
    forward(0, 1)
    line_next(0, 3)
    start("pass", 0, OWN)
    narrow_next(0, 1)
    forward(0, 2)
    narrow_next(0, 2)
    forward(0, 3)
    narrow_next(0, 3)
    begin(1)
    start("pass_narrow", 0, 0)
    gather(0, OWN)
    pass_x(0)
    pass_y(0)
    spread(1, z)
    gather(0, FLIP_X)
    pass_both(0)
    gather(0, FLIP_Y)
    line_next(1, 1)
    gather(0, FLIP_BOTH)
    gather_narrow(0)
    for copy in weight_copies:
        copy.wait()

    def beside_first(i):
        @pl.when(i == 0)
        def _():
            plane_next(1)

        @pl.when(i > 0)
        def _():
            forward(1, i - 1)

        @pl.when((i == 1) | (i == 2))
        def _():
            line_next(1, i + 1)

    run_experts(beside_first)
    start("pass", 1, OWN)
    narrow_next(1, 1)
    forward(1, 3)
    combine(0, FLIP_BOTH)
    narrow_next(1, 2)
    combine(0, FLIP_X)
    send_both(0)
    pass_x(1)
    combine(0, FLIP_Y)
    narrow_next(1, 3)
    arrive("share", 0, FLIP_X)
    combine(0, OWN)
    arrive("share", 0, FLIP_Y)
    turn(0, late[0])
    pass_y(1)
    start("pass_narrow", 1, 0)
    gather(1, OWN)
    turn(0, late[1])
    send_narrow(0)
    gather(1, FLIP_X)
    turn(0, late[2])
    pass_both(1)
    gather(1, FLIP_Y)
    turn(0, late[3])
    gather(1, FLIP_BOTH)
    gather_narrow(1)

    def finish_line(w, k):
        finish(w, k)
        if k:
            start("line_end", w, k)

    def beside_second(i):
        @pl.when(i == 1)
        def _():
            turn_narrow(0)

        @pl.when(i == 2)
        def _():
            finish_line(0, late[0])

        @pl.when(i == 3)
        def _():
            finish_line(0, late[1])

    run_experts(beside_second)
    combine(1, FLIP_BOTH)
    finish_line(0, late[2])
    combine(1, FLIP_X)
    send_both(1)
    combine(1, FLIP_Y)
    finish_line(0, late[3])
    arrive("share", 1, FLIP_X)
    combine(1, OWN)
    arrive("share", 1, FLIP_Y)
    turn(1, late[0])
    turn(1, late[1])
    send_narrow(1)
    turn(1, late[2])
    finish_line(1, late[0])
    turn(1, late[3])
    turn_narrow(1)
    conclude(0)
    finish_line(1, late[1])
    finish_line(1, late[2])
    finish_line(1, late[3])
    conclude(1)
    hand_over = remote(2 * STRIDE + 1, done.at[1 - core], got, sibling)
    hand_over.start()
    gain = gain_ref[...].astype(jnp.float32)

    def finalize(total, part):
        span = pl.ds(pl.multiple_of(part * half, half), half)
        total = total + mixed_ref[span]
        mean_square = jnp.mean(total * total, axis=-1, keepdims=True)
        out_ref[span] = (total * lax.rsqrt(mean_square + epsilon) * gain).astype(jnp.bfloat16)

    finalize(done[core], core)
    hand_over.wait_recv()
    finalize(got[...], 1 - core)
    hand_over.wait_send()
    exchange.wait_send()
    skip = ("plane", "line_end", "back_line", "back_plane")
    moves = {"right": -1, "left": 1, "plane_right": -1, "plane_left": 1}
    for w in range(2):
        for name, count in COUNTS:
            if name in moves:
                for k in range(LINE - 1):
                    if moves[name] < 0:
                        sent = (z >= k) & (z < LINE - 1)
                    else:
                        sent = (z + k < LINE) & (z > 0)

                    @pl.when(sent)
                    def _():
                        copy_of(name, w, k).wait_send()
            else:
                for k in range(1 if name in skip else 0, count):
                    copy_of(name, w, k).wait_send()


def waves(
    context, residual, out_proj, attn_gain, router, expert_ids,
    gate_weight, up_weight, down_weight, final_gain,
):
    row_count, width = context.shape
    mixed_stream, normed, weights = front(
        context, residual, out_proj, attn_gain, router, expert_ids
    )
    top = weights.astype(jnp.bfloat16)
    block = jnp.concatenate([normed, top, jnp.zeros_like(top)], axis=1)
    half = row_count // 2
    quarter = half // 2
    local = gate_weight.shape[0]
    slots = LINE * capacity
    chunk = 2 * LINE * half
    rest = width - BACK_ACROSS
    low = jnp.bfloat16
    vmem = pl.BlockSpec(memory_space=pltpu.VMEM)
    hbm = pl.BlockSpec(memory_space=pl.ANY)
    return pl.pallas_call(
        wave_kernel,
        out_shape=jax.ShapeDtypeStruct((row_count, width), low),
        in_specs=[vmem, vmem, vmem, hbm, hbm, hbm],
        out_specs=vmem,
        scratch_shapes=[
            pltpu.VMEM((2, 4, LINE, 2, half, block.shape[1]), low),
            pltpu.VMEM(gate_weight.shape, low),
            pltpu.VMEM(up_weight.shape, low),
            pltpu.VMEM(down_weight.shape, low),
            pltpu.VMEM((local, 4 * slots, width), low),
            pltpu.VMEM((4, local, slots, chunk), low),
            pltpu.VMEM((4, local, slots, chunk), low),
            pltpu.VMEM((2, 4, 2, LINE, half, width), low),
            pltpu.VMEM((2, 4, LINE, half, width), low),
            pltpu.VMEM((2, 2, LINE, quarter, rest), low),
            pltpu.VMEM((2, 2, LINE, quarter, rest), low),
            pltpu.VMEM((2, 2, LINE, quarter, rest), low),
            pltpu.VMEM((2, LINE - 1, half, rest), low),
            pltpu.VMEM((2, LINE - 1, 4, half, BACK_ACROSS), low),
            pltpu.VMEM((2, 3, half, BACK_ACROSS), low),
            pltpu.VMEM((2, half, width), jnp.float32),
            pltpu.VMEM((half, width), jnp.float32),
            pltpu.SemaphoreType.DMA((3,)),
            pltpu.SemaphoreType.DMA((COPIES,)),
            pltpu.SemaphoreType.DMA((COPIES,)),
        ],
        compiler_params=pltpu.CompilerParams(
            collective_id=0, has_side_effects=True, vmem_limit_bytes=63 * 1024 * 1024
        ),
    )(block, mixed_stream, final_gain.reshape(1, width), gate_weight, up_weight, down_weight)


def solution(mesh):
    per_device = waves if dict(mesh.shape) == {"ep": 2 * LINE, "rep": 4} else gathered
    in_specs = (
        P(("ep", "rep"), None),
        P(("ep", "rep"), None),
        P(),
        P(),
        P(),
        P(("ep", "rep"), None),
        P("ep", None, "rep"),
        P("ep", None, "rep"),
        P("ep", None, "rep"),
        P(),
    )
    out_specs = P(("ep", "rep"), None)
    return jax.shard_map(
        per_device, mesh=mesh, in_specs=in_specs, out_specs=out_specs, check_vma=False
    )
```

```python
import functools

import jax
import jax.numpy as jnp
from jax import lax
from jax.experimental import pallas as pl
from jax.experimental.pallas import tpu as pltpu
from jax.sharding import PartitionSpec as P

epsilon = 1e-05
capacity = 16


def rms_scale(values, gain_vector):
    mean_square = jnp.mean(values * values, axis=-1, keepdims=True)
    return values * lax.rsqrt(mean_square + epsilon) * gain_vector.astype(jnp.float32)


def front(context, residual, out_proj, attn_gain, router, expert_ids):
    expert_count = router.shape[1]
    attention = jnp.dot(context, out_proj, preferred_element_type=jnp.float32)
    mixed_stream = residual.astype(jnp.float32) + attention
    normed = rms_scale(mixed_stream, attn_gain).astype(jnp.bfloat16)
    logits = jnp.dot(normed, router, preferred_element_type=jnp.float32)
    probs = jax.nn.softmax(logits, axis=1)
    chosen = jnp.any(
        expert_ids[:, :, None] == jnp.arange(expert_count, dtype=jnp.int32)[None, None, :], axis=1
    )
    weights = jnp.where(chosen, probs, 0.0)
    return mixed_stream, normed, weights


def gathered(
    context, residual, out_proj, attn_gain, router, expert_ids,
    gate_weight, up_weight, down_weight, final_gain,
):
    row_count, model_width = context.shape
    local_experts = gate_weight.shape[0]
    owners = lax.axis_size("ep")
    sources = owners * lax.axis_size("rep")
    mixed_stream, normed, weights = front(
        context, residual, out_proj, attn_gain, router, expert_ids
    )
    high = weights.astype(jnp.bfloat16)
    low = (weights - high.astype(jnp.float32)).astype(jnp.bfloat16)
    block = jnp.concatenate([normed, high, low], axis=1)
    everyone = lax.all_gather(block, ("ep", "rep"), axis=0, tiled=False)
    rows = everyone[:, :, :model_width]
    first = model_width + lax.axis_index("ep") * local_experts
    high = lax.dynamic_slice_in_dim(everyone, first, local_experts, axis=2)
    low = lax.dynamic_slice_in_dim(everyone, first + weights.shape[1], local_experts, axis=2)
    local_weights = high.astype(jnp.float32) + low.astype(jnp.float32)
    mask = (local_weights > 0).astype(jnp.float32)
    earlier = (
        jnp.arange(row_count)[:, None] > jnp.arange(row_count)[None, :]
    ).astype(jnp.float32)
    rank = jnp.einsum("ij,sje->sie", earlier, mask)
    slots = jnp.arange(capacity, dtype=jnp.float32)
    placing = jnp.where(
        (rank[:, :, :, None] == slots) & (mask[:, :, :, None] > 0), 1.0, 0.0
    )
    slot_weight = jnp.sum(placing * local_weights[:, :, :, None], axis=1)
    placing = placing.astype(jnp.bfloat16).reshape(sources, row_count, local_experts * capacity)
    grouped = jnp.einsum(
        "sit,sid->std", placing, rows, preferred_element_type=jnp.float32
    ).astype(jnp.bfloat16)
    grouped = grouped.reshape(sources, local_experts, capacity, model_width)
    gate_proj = jnp.einsum(
        "serd,edw->serw", grouped, gate_weight, preferred_element_type=jnp.float32
    )
    up_proj = jnp.einsum("serd,edw->serw", grouped, up_weight, preferred_element_type=jnp.float32)
    active = (jax.nn.silu(gate_proj) * up_proj * slot_weight[..., None]).astype(jnp.bfloat16)
    part = jnp.einsum(
        "serw,edw->serd", active, down_weight, preferred_element_type=jnp.float32
    ).astype(jnp.bfloat16)
    part = part.reshape(sources, local_experts * capacity, model_width)
    share = jnp.einsum("sit,std->sid", placing, part, preferred_element_type=jnp.float32)
    share = share.astype(jnp.bfloat16).reshape(sources * row_count, model_width)
    expert_mix = lax.psum_scatter(share, ("ep", "rep"), scatter_dimension=0, tiled=True)
    total = mixed_stream + expert_mix.astype(jnp.float32)
    return rms_scale(total, final_gain).astype(jnp.bfloat16)


MESH = pl.DeviceIdType.MESH
LINE = 4
OWN, FLIP_X, FLIP_Y, FLIP_BOTH = 0, 1, 2, 3
GO_ACROSS, BACK_ACROSS = 256, 256
COUNTS = (
    ("right", LINE), ("left", LINE), ("x_low", LINE), ("x_high", LINE), ("y_low", LINE),
    ("y_high", LINE), ("far_low", LINE), ("far_high", LINE), ("pass", 4), ("pass_narrow", 1),
    ("plane", 4), ("plane_right", LINE), ("plane_left", LINE),
    ("share", 4), ("y_first", LINE), ("x_first", LINE), ("x_next", LINE), ("y_next", LINE),
    ("x_last", LINE), ("y_last", LINE), ("line_end", LINE), ("back_line", LINE), ("back_plane", 4),
)
BASE = {name: sum(count for _, count in COUNTS[:i]) for i, (name, _) in enumerate(COUNTS)}
STRIDE = sum(count for _, count in COUNTS)
COPIES = 2 * STRIDE + 2


def wave_kernel(
    context_ref, residual_ref, attn_gain_ref, router_ref, ids_ref, gain_ref,
    proj_hbm, gate_hbm, up_hbm, down_hbm, out_ref, block, mixed, rows, gate, up, down, grouped, hits, weighted,
    comb, sib, first, follow, final, line_sum, back_line, back_plane, done, got,
    proj_sem, weight_sem, send_sem, recv_sem,
):
    half = block.shape[0] // 2
    quarter = half // 2
    width = mixed.shape[1]
    extra = block.shape[1] - width
    expert_count = router_ref.shape[0]
    piece = down.shape[2]
    local = gate.shape[0]
    chunk = 2 * LINE * half
    slots = LINE * capacity
    tile = 512

    ep, rep = lax.axis_index("ep"), lax.axis_index("rep")
    z, x, y, core = ep // 2, ep % 2, rep // 2, rep % 2
    across_x = (z * 2 + (1 - x), rep)
    across_y = (ep, (1 - y) * 2 + core)
    diagonal = (z * 2 + (1 - x), (1 - y) * 2 + core)
    sibling = (ep, y * 2 + (1 - core))
    planes = {FLIP_X: across_x, FLIP_Y: across_y, FLIP_BOTH: diagonal}

    def along_z(step):
        return (((z + step) % LINE) * 2 + x, rep)

    peers = [across_x, across_y, diagonal, sibling] + [along_z(step) for step in (1, 2, 3)]
    barrier = pltpu.get_barrier_semaphore()
    for peer in peers:
        pl.semaphore_signal(barrier, inc=1, device_id=peer, device_id_type=MESH)
    weight_copies = [
        pltpu.make_async_copy(source, target, weight_sem.at[i])
        for i, (source, target) in enumerate(((gate_hbm, gate), (up_hbm, up), (down_hbm, down)))
    ]
    proj_copies = [
        pltpu.make_async_copy(
            proj_hbm.at[:, pl.ds(i * piece, piece)], down.at[i], proj_sem.at[i]
        )
        for i in range(width // piece)
    ]
    for copy in proj_copies:
        copy.start()

    slim = pl.ds(0, GO_ACROSS)
    wide = pl.ds(GO_ACROSS, width + extra - GO_ACROSS)
    narrow = pl.ds(0, BACK_ACROSS)
    body = pl.ds(BACK_ACROSS, width - BACK_ACROSS)
    low, high = pl.ds(0, quarter), pl.ds(quarter, quarter)

    def remote(index, source, target, device):
        return pltpu.make_async_remote_copy(
            src_ref=source, dst_ref=target, send_sem=send_sem.at[index],
            recv_sem=recv_sem.at[index], device_id=device, device_id_type=MESH,
        )

    def column(k):
        return (z + k) % LINE

    tours = tuple(
        sum(place * LINE**i for i, place in enumerate(tour))
        for tour in ((0, 1, 2, 3), (1, 0, 2, 3), (2, 3, 1, 0), (3, 2, 1, 0))
    )
    tour = jnp.where(z < 2, jnp.where(z == 0, *tours[:2]), jnp.where(z == 2, *tours[2:]))

    def stop(n):
        power = 1
        for i in range(1, LINE):
            power = power * (1 + (LINE - 1) * jnp.where(n >= i, 1, 0))
        return (tour // power) % LINE

    def copy_of(name, w, k):
        index = w * STRIDE + BASE[name] + k
        if name == "right":
            at = rows.at[w, OWN, (z - k + LINE) % LINE, core, :, wide]
            pair = at, at, along_z(1)
        elif name == "left":
            at = rows.at[w, OWN, (z + k) % LINE, core, :, wide]
            pair = at, at, along_z(LINE - 1)
        elif name == "plane_right":
            at = rows.at[w, :, (z - k + LINE) % LINE, core, :, slim]
            pair = at, at, along_z(1)
        elif name == "plane_left":
            at = rows.at[w, :, (z + k) % LINE, core, :, slim]
            pair = at, at, along_z(LINE - 1)
        elif name in ("x_low", "x_high"):
            part = low if name == "x_low" else high
            pair = (
                rows.at[w, OWN, k, core, part, wide], rows.at[w, FLIP_X, k, core, part, wide],
                across_x,
            )
        elif name in ("y_low", "y_high"):
            part = low if name == "y_low" else high
            pair = (
                rows.at[w, OWN, k, core, part, wide], rows.at[w, FLIP_Y, k, core, part, wide],
                across_y,
            )
        elif name == "far_low":
            pair = (
                rows.at[w, FLIP_X, k, core, low, wide], rows.at[w, FLIP_BOTH, k, core, low, wide],
                across_y,
            )
        elif name == "far_high":
            pair = (
                rows.at[w, FLIP_Y, k, core, high, wide],
                rows.at[w, FLIP_BOTH, k, core, high, wide], across_x,
            )
        elif name == "pass":
            at = rows.at[w, k, :, core, :, wide]
            pair = at, at, sibling
        elif name == "pass_narrow":
            at = rows.at[w, :, :, core, :, slim]
            pair = at, at, sibling
        elif name == "plane":
            pair = rows.at[w, OWN, z, core, :, slim], rows.at[w, k, z, core, :, slim], planes[k]
        elif name == "share":
            pair = comb.at[w, k, 1 - core], sib.at[w, k], sibling
        elif name == "y_first":
            pair = comb.at[w, FLIP_BOTH, core, column(k), low, body], first.at[w, 0, k], across_y
        elif name == "x_first":
            pair = comb.at[w, FLIP_BOTH, core, column(k), high, body], first.at[w, 1, k], across_x
        elif name == "x_next":
            pair = comb.at[w, FLIP_X, core, column(k), high, body], follow.at[w, 1, k], across_x
        elif name == "y_next":
            pair = comb.at[w, FLIP_Y, core, column(k), low, body], follow.at[w, 0, k], across_y
        elif name == "x_last":
            pair = comb.at[w, FLIP_X, core, column(k), low, body], final.at[w, 0, k], across_x
        elif name == "y_last":
            pair = comb.at[w, FLIP_Y, core, column(k), high, body], final.at[w, 1, k], across_y
        elif name == "line_end":
            pair = (
                comb.at[w, OWN, core, column(k), :, body], line_sum.at[w, k - 1], along_z(k)
            )
        elif name == "back_line":
            pair = comb.at[w, :, core, column(k), :, narrow], back_line.at[w, k - 1], along_z(k)
        elif name == "back_plane":
            pair = comb.at[w, k, core, z, :, narrow], back_plane.at[w, k - 1], planes[k]
        return remote(index, *pair)

    def start(name, w, k):
        copy_of(name, w, k).start()

    def arrive(name, w, k):
        copy_of(name, w, k).wait_recv()

    def spread(w, k):
        for name in ("x_low", "y_high", "y_low", "x_high"):
            start(name, w, k)

    def start_line(w, right, left):
        pl.when(z < LINE - 1)(lambda: start(right, w, 0))
        pl.when(z > 0)(lambda: start(left, w, 0))

    def begin(w):
        for k in (FLIP_X, FLIP_Y, FLIP_BOTH):
            start("plane", w, k)
        start_line(w, "right", "left")

    def plane_next(w):
        for k in (FLIP_X, FLIP_Y, FLIP_BOTH):
            arrive("plane", w, k)
        start_line(w, "plane_right", "plane_left")

    def along(w, n, right, left, at):
        source = stop(n)
        index = w * STRIDE + jnp.where(
            source < z, BASE[right] + z - source - 1, BASE[left] + source - z - 1
        )
        remote(index, at(source), at(source), across_x).wait_recv()
        pl.when((source < z) & (z < LINE - 1))(lambda: start(right, w, z - source))
        pl.when((source > z) & (z > 0))(lambda: start(left, w, source - z))
        return source

    def line_next(w, n):
        spread(w, along(w, n, "right", "left", lambda k: rows.at[w, OWN, k, core, :, wide]))

    def narrow_next(w, n):
        along(w, n, "plane_right", "plane_left", lambda k: rows.at[w, :, k, core, :, slim])

    def forward(w, n):
        k = stop(n)
        arrive("x_low", w, k)
        start("far_low", w, k)
        arrive("y_high", w, k)
        start("far_high", w, k)

    def pass_x(w):
        for k in range(LINE):
            arrive("x_high", w, k)
        start("pass", w, FLIP_X)

    def pass_y(w):
        for k in range(LINE):
            arrive("y_low", w, k)
        start("pass", w, FLIP_Y)

    def pass_both(w):
        for k in range(LINE):
            arrive("far_low", w, k)
            arrive("far_high", w, k)
        start("pass", w, FLIP_BOTH)

    column_of = lax.broadcasted_iota(jnp.int32, (16, extra), 1)
    wanted = lax.broadcasted_iota(jnp.int32, (16, extra), 0)
    pick = jnp.where((column_of == ep * local + wanted) & (wanted < local), 1.0, 0.0).astype(
        jnp.bfloat16
    )
    above = lax.broadcasted_iota(jnp.int32, (chunk, chunk), 0)
    below = lax.broadcasted_iota(jnp.int32, (chunk, chunk), 1)
    earlier = jnp.where(
        (above < below) & (above // (2 * half) == below // (2 * half)), 1.0, 0.0
    ).astype(jnp.bfloat16)
    start_slot = (
        (lax.broadcasted_iota(jnp.int32, (16, chunk), 1) // (2 * half)) * capacity
    ).astype(jnp.float32)
    slot_number = lax.broadcasted_iota(jnp.int32, (slots, chunk), 0).astype(jnp.float32)

    def gather(w, place):
        arrive("pass", w, place)
        packed = rows[w, place, :, :, :, width:].reshape(chunk, extra)
        weight = lax.dot_general(
            pick, packed, (((1,), (1,)), ((), ())), preferred_element_type=jnp.float32
        )
        mask = jnp.where(weight > 0, 1.0, 0.0)
        rank = jnp.dot(mask.astype(jnp.bfloat16), earlier, preferred_element_type=jnp.float32)
        target = jnp.where(mask > 0, start_slot + rank, -1.0)
        for e in range(local):
            hit = target[e : e + 1, :] == slot_number
            hits[place, e] = jnp.where(hit, 1.0, 0.0).astype(jnp.bfloat16)
            weighted[place, e] = jnp.where(hit, weight[e : e + 1, :], 0.0).astype(jnp.bfloat16)
        fill(w, place, pl.ds(GO_ACROSS, width - GO_ACROSS))

    def fill(w, place, span):
        found = jnp.dot(
            hits[place].reshape(local * slots, chunk),
            rows[w, place, :, :, :, span].reshape(chunk, span.size),
            preferred_element_type=jnp.float32,
        )
        grouped[:, place * slots : (place + 1) * slots, span] = found.astype(
            jnp.bfloat16
        ).reshape(local, slots, span.size)

    def gather_narrow(w):
        arrive("pass_narrow", w, 0)
        for place in range(4):
            fill(w, place, slim)

    def run_experts(beside):
        @pl.loop(0, local // 2)
        def _(i):
            beside(i)
            active = []
            for e in (2 * i, 2 * i + 1):
                batch = grouped[e]
                gate_proj = jnp.dot(batch, gate[e], preferred_element_type=jnp.float32)
                up_proj = jnp.dot(batch, up[e], preferred_element_type=jnp.float32)
                value = gate_proj / (1.0 + jnp.exp(-gate_proj)) * up_proj
                active.append(value.astype(jnp.bfloat16))
            for e, value in zip((2 * i, 2 * i + 1), active):
                for t in range(width // tile):
                    part = lax.dot_general(
                        value, down[e, t * tile : (t + 1) * tile, :], (((1,), (1,)), ((), ())),
                        preferred_element_type=jnp.float32,
                    )
                    grouped[e, :, t * tile : (t + 1) * tile] = part.astype(jnp.bfloat16)

    def combine(w, place):
        table = weighted[place].reshape(local * slots, chunk)
        piece = grouped[:, place * slots : (place + 1) * slots, :].reshape(local * slots, width)
        result = lax.dot_general(
            table, piece, (((0,), (0,)), ((), ())), preferred_element_type=jnp.float32
        ).astype(jnp.bfloat16).reshape(LINE, 2, half, width)
        for part in range(2):
            comb[w, place, part] = result[:, part]
        start("share", w, place)

    def add_into(target, *terms):
        total = target[...].astype(jnp.float32)
        for term in terms:
            total = total + term[...].astype(jnp.float32)
        target[...] = total.astype(jnp.bfloat16)

    def mine(w, place, k, part, span):
        return comb.at[w, place, core, column(k), part, span]

    def theirs(w, place, k, part, span):
        return sib.at[w, place, column(k), part, span]

    every = pl.ds(0, half)

    def send_both(w):
        arrive("share", w, FLIP_BOTH)
        for k in late:
            add_into(
                mine(w, FLIP_BOTH, k, every, body), theirs(w, FLIP_BOTH, k, every, body)
            )
            start("y_first", w, k)
            start("x_first", w, k)

    def send_narrow(w):
        arrive("share", w, OWN)
        for k in late[:-1]:
            for place in range(4):
                add_into(mine(w, place, k, every, narrow), theirs(w, place, k, every, narrow))
            start("back_line", w, k)

    def turn(w, k):
        arrive("y_first", w, k)
        add_into(
            mine(w, FLIP_X, k, low, body), theirs(w, FLIP_X, k, low, body), first.at[w, 0, k]
        )
        start("x_last", w, k)
        arrive("x_first", w, k)
        add_into(
            mine(w, FLIP_Y, k, high, body), theirs(w, FLIP_Y, k, high, body), first.at[w, 1, k]
        )
        start("y_last", w, k)
        add_into(mine(w, FLIP_X, k, high, body), theirs(w, FLIP_X, k, high, body))
        start("x_next", w, k)
        add_into(mine(w, FLIP_Y, k, low, body), theirs(w, FLIP_Y, k, low, body))
        start("y_next", w, k)

    def turn_narrow(w):
        for k in late[:-1]:
            arrive("back_line", w, k)
        for place in (FLIP_BOTH, FLIP_X, FLIP_Y, OWN):
            add_into(
                mine(w, place, 0, every, narrow), theirs(w, place, 0, every, narrow),
                *(back_line.at[w, k, place] for k in range(LINE - 1)),
            )
            if place != OWN:
                start("back_plane", w, place)

    def finish(w, k):
        arrive("y_next", w, k)
        arrive("x_last", w, k)
        add_into(
            mine(w, OWN, k, low, body), theirs(w, OWN, k, low, body),
            follow.at[w, 0, k], final.at[w, 0, k],
        )
        arrive("x_next", w, k)
        arrive("y_last", w, k)
        add_into(
            mine(w, OWN, k, high, body), theirs(w, OWN, k, high, body),
            follow.at[w, 1, k], final.at[w, 1, k],
        )

    def conclude(w):
        for k in late[:-1]:
            arrive("line_end", w, k)
        for place in (FLIP_X, FLIP_Y, FLIP_BOTH):
            arrive("back_plane", w, place)
        total = comb[w, OWN, core, z, :, body].astype(jnp.float32)
        for k in range(LINE - 1):
            total = total + line_sum[w, k].astype(jnp.float32)
        done[w, :, body] = total
        total = comb[w, OWN, core, z, :, narrow].astype(jnp.float32)
        for k in range(3):
            total = total + back_plane[w, k].astype(jnp.float32)
        done[w, :, narrow] = total

    late = (2, 1, 3, 0)
    skip = ("plane", "line_end", "back_line", "back_plane")
    moves = {"right": -1, "left": 1, "plane_right": -1, "plane_left": 1}
    ends = (
        "y_first", "x_first", "x_next", "y_next", "x_last", "y_last", "line_end", "back_line",
        "back_plane",
    )

    def drain(w, names):
        for name, count in COUNTS:
            if name not in names:
                continue
            for k in range(LINE - 1 if name in moves else count):
                if name in moves:
                    sent = (z > 0) & (z + k < LINE)
                    if moves[name] < 0:
                        sent = (z >= k) & (z < LINE - 1)
                    pl.when(sent)(functools.partial(lambda n, i: copy_of(n, w, i).wait_send(), name, k))
                elif k or name not in skip:
                    copy_of(name, w, k).wait_send()

    square = jnp.zeros((2 * half, 1), jnp.float32)
    for i, copy in enumerate(proj_copies):
        copy.wait()
        if i in (1, 3):
            weight_copies[i // 2].start()
        span = pl.ds(i * piece, piece)
        stream = residual_ref[:, span].astype(jnp.float32) + jnp.dot(
            context_ref[...], down[i], preferred_element_type=jnp.float32
        )
        mixed[:, span] = stream
        square = square + jnp.sum(stream * stream, axis=1, keepdims=True)
    scale = lax.rsqrt(square * (1.0 / width) + epsilon)
    normed = (mixed[...] * scale * attn_gain_ref[...].astype(jnp.float32).reshape(1, width)).astype(jnp.bfloat16)
    block[:, :width] = normed
    logits = lax.dot_general(
        normed, router_ref[...], (((1,), (1,)), ((), ())), preferred_element_type=jnp.float32
    )
    raised = jnp.exp(logits - jnp.max(logits, axis=1, keepdims=True))
    probs = raised / jnp.sum(raised, axis=1, keepdims=True)
    expert = lax.broadcasted_iota(jnp.int32, (expert_count, 2 * half), 0)
    named = ids_ref[0:1, :] == expert
    for i in range(1, ids_ref.shape[0]):
        named = named | (ids_ref[i : i + 1, :] == expert)
    unit = jnp.where(
        lax.broadcasted_iota(jnp.int32, (2 * half, 2 * half), 0)
        == lax.broadcasted_iota(jnp.int32, (2 * half, 2 * half), 1), 1.0, 0.0
    ).astype(jnp.bfloat16)
    chosen = lax.dot_general(
        unit, jnp.where(named, 1.0, 0.0).astype(jnp.bfloat16), (((1,), (1,)), ((), ())),
        preferred_element_type=jnp.float32,
    )
    block[:, width : width + expert_count] = jnp.where(chosen > 0.5, probs, 0.0).astype(
        jnp.bfloat16
    )
    block[:, width + expert_count :] = jnp.zeros((2 * half, extra - expert_count), jnp.bfloat16)
    pl.semaphore_wait(barrier, len(peers))
    rows[core, OWN, z, core] = block[pl.ds(pl.multiple_of(core * half, half), half)]
    given = block.at[pl.ds(pl.multiple_of((1 - core) * half, half), half)]
    taken = rows.at[1 - core, OWN, z, core]
    exchange = remote(2 * STRIDE, given, rows.at[core, OWN, z, 1 - core], sibling)
    exchange.start()
    remote(2 * STRIDE, taken, taken, sibling).wait_recv()

    begin(0)
    spread(0, z)
    line_next(0, 1)
    inner = (z > 0) & (z < LINE - 1)
    pl.when(inner)(lambda: line_next(0, 2))
    plane_next(0)
    forward(0, 0)
    pl.when(~inner)(lambda: line_next(0, 2))
    forward(0, 1)
    line_next(0, 3)
    start("pass", 0, OWN)
    narrow_next(0, 1)
    forward(0, 2)
    narrow_next(0, 2)
    forward(0, 3)
    weight_copies[2].start()
    narrow_next(0, 3)
    begin(1)
    start("pass_narrow", 0, 0)
    gather(0, OWN)
    pass_x(0)
    pass_y(0)
    spread(1, z)
    gather(0, FLIP_X)
    pass_both(0)
    gather(0, FLIP_Y)
    line_next(1, 1)
    gather(0, FLIP_BOTH)
    gather_narrow(0)
    for copy in weight_copies:
        copy.wait()

    def beside_first(i):
        @pl.when(i == 1)
        def _():
            plane_next(1)
            forward(1, 0)

        @pl.when(i >= 2)
        def _():
            line_next(1, i)

        @pl.when(i == 3)
        def _():
            forward(1, 1)

    run_experts(beside_first)
    start("pass", 1, OWN)
    narrow_next(1, 1)
    forward(1, 2)
    combine(0, FLIP_BOTH)
    forward(1, 3)
    narrow_next(1, 2)
    combine(0, FLIP_X)
    send_both(0)
    pass_x(1)
    combine(0, FLIP_Y)
    narrow_next(1, 3)
    arrive("share", 0, FLIP_X)
    combine(0, OWN)
    arrive("share", 0, FLIP_Y)
    turn(0, late[0])
    pass_y(1)
    start("pass_narrow", 1, 0)
    gather(1, OWN)
    turn(0, late[1])
    send_narrow(0)
    gather(1, FLIP_X)
    turn(0, late[2])
    pass_both(1)
    gather(1, FLIP_Y)
    turn(0, late[3])
    gather(1, FLIP_BOTH)
    gather_narrow(1)

    def finish_line(w, k):
        finish(w, k)
        if k:
            start("line_end", w, k)

    def beside_second(i):
        @pl.when(i == 2)
        def _():
            turn_narrow(0)

        @pl.when(i == 3)
        def _():
            finish_line(0, late[0])

    run_experts(beside_second)
    combine(1, FLIP_BOTH)
    finish_line(0, late[1])
    combine(1, FLIP_X)
    finish_line(0, late[2])
    send_both(1)
    combine(1, FLIP_Y)
    finish_line(0, late[3])
    arrive("share", 1, FLIP_X)
    combine(1, OWN)
    arrive("share", 1, FLIP_Y)
    turn(1, late[0])
    turn(1, late[1])
    send_narrow(1)
    turn(1, late[2])
    drain(0, [name for name, _ in COUNTS])
    drain(1, [name for name, _ in COUNTS if name not in ends])
    exchange.wait_send()
    finish_line(1, late[0])
    turn(1, late[3])
    turn_narrow(1)
    conclude(0)
    finish_line(1, late[1])
    finish_line(1, late[2])
    finish_line(1, late[3])
    conclude(1)
    hand_over = remote(2 * STRIDE + 1, done.at[1 - core], got, sibling)
    hand_over.start()
    gain = gain_ref[...].astype(jnp.float32).reshape(1, width)

    def finalize(total, part):
        span = pl.ds(pl.multiple_of(part * half, half), half)
        total = total + mixed[span]
        mean_square = jnp.mean(total * total, axis=-1, keepdims=True)
        out_ref[span] = (total * lax.rsqrt(mean_square + epsilon) * gain).astype(jnp.bfloat16)

    finalize(done[core], core)
    hand_over.wait_recv()
    finalize(got[...], 1 - core)
    hand_over.wait_send()
    drain(1, ends)


def waves(
    context, residual, out_proj, attn_gain, router, expert_ids,
    gate_weight, up_weight, down_weight, final_gain,
):
    row_count, width = context.shape
    padded = width + 2 * router.shape[1]
    half = row_count // 2
    quarter = half // 2
    local = gate_weight.shape[0]
    slots = LINE * capacity
    chunk = 2 * LINE * half
    rest = width - BACK_ACROSS
    low = jnp.bfloat16
    vmem = pl.BlockSpec(memory_space=pltpu.VMEM)
    hbm = pl.BlockSpec(memory_space=pl.ANY)
    return pl.pallas_call(
        wave_kernel,
        out_shape=jax.ShapeDtypeStruct((row_count, width), low),
        in_specs=[vmem] * 6 + [hbm] * 4,
        out_specs=vmem,
        scratch_shapes=[
            pltpu.VMEM((row_count, padded), low),
            pltpu.VMEM((row_count, width), jnp.float32),
            pltpu.VMEM((2, 4, LINE, 2, half, padded), low),
            pltpu.VMEM(gate_weight.shape, low),
            pltpu.VMEM(up_weight.shape, low),
            pltpu.VMEM(down_weight.shape, low),
            pltpu.VMEM((local, 4 * slots, width), low),
            pltpu.VMEM((4, local, slots, chunk), low),
            pltpu.VMEM((4, local, slots, chunk), low),
            pltpu.VMEM((2, 4, 2, LINE, half, width), low),
            pltpu.VMEM((2, 4, LINE, half, width), low),
            pltpu.VMEM((2, 2, LINE, quarter, rest), low),
            pltpu.VMEM((2, 2, LINE, quarter, rest), low),
            pltpu.VMEM((2, 2, LINE, quarter, rest), low),
            pltpu.VMEM((2, LINE - 1, half, rest), low),
            pltpu.VMEM((2, LINE - 1, 4, half, BACK_ACROSS), low),
            pltpu.VMEM((2, 3, half, BACK_ACROSS), low),
            pltpu.VMEM((2, half, width), jnp.float32),
            pltpu.VMEM((half, width), jnp.float32),
            pltpu.SemaphoreType.DMA((width // down_weight.shape[2],)),
            pltpu.SemaphoreType.DMA((3,)),
            pltpu.SemaphoreType.DMA((COPIES,)),
            pltpu.SemaphoreType.DMA((COPIES,)),
        ],
        compiler_params=pltpu.CompilerParams(
            collective_id=0, has_side_effects=True, vmem_limit_bytes=63 * 1024 * 1024
        ),
    )(
        context, residual, attn_gain, router.T, expert_ids.T, final_gain, out_proj,
        gate_weight, up_weight, down_weight,
    )


def solution(mesh):
    per_device = waves if dict(mesh.shape) == {"ep": 2 * LINE, "rep": 4} else gathered
    in_specs = (
        P(("ep", "rep"), None),
        P(("ep", "rep"), None),
        P(),
        P(),
        P(),
        P(("ep", "rep"), None),
        P("ep", None, "rep"),
        P("ep", None, "rep"),
        P("ep", None, "rep"),
        P(),
    )
    out_specs = P(("ep", "rep"), None)
    return jax.shard_map(
        per_device, mesh=mesh, in_specs=in_specs, out_specs=out_specs, check_vma=False
    )
```

```python
import functools

import jax
import jax.numpy as jnp
from jax import lax
from jax.experimental import pallas as pl
from jax.experimental.pallas import tpu as pltpu
from jax.sharding import PartitionSpec as P

epsilon = 1e-05
capacity = 16


def rms_scale(values, gain_vector):
    mean_square = jnp.mean(values * values, axis=-1, keepdims=True)
    return values * lax.rsqrt(mean_square + epsilon) * gain_vector.astype(jnp.float32)


def front(context, residual, out_proj, attn_gain, router, expert_ids):
    expert_count = router.shape[1]
    attention = jnp.dot(context, out_proj, preferred_element_type=jnp.float32)
    mixed_stream = residual.astype(jnp.float32) + attention
    normed = rms_scale(mixed_stream, attn_gain).astype(jnp.bfloat16)
    logits = jnp.dot(normed, router, preferred_element_type=jnp.float32)
    probs = jax.nn.softmax(logits, axis=1)
    chosen = jnp.any(
        expert_ids[:, :, None] == jnp.arange(expert_count, dtype=jnp.int32)[None, None, :], axis=1
    )
    weights = jnp.where(chosen, probs, 0.0)
    return mixed_stream, normed, weights


def gathered(
    context, residual, out_proj, attn_gain, router, expert_ids,
    gate_weight, up_weight, down_weight, final_gain,
):
    row_count, model_width = context.shape
    local_experts = gate_weight.shape[0]
    owners = lax.axis_size("ep")
    sources = owners * lax.axis_size("rep")
    mixed_stream, normed, weights = front(
        context, residual, out_proj, attn_gain, router, expert_ids
    )
    high = weights.astype(jnp.bfloat16)
    low = (weights - high.astype(jnp.float32)).astype(jnp.bfloat16)
    block = jnp.concatenate([normed, high, low], axis=1)
    everyone = lax.all_gather(block, ("ep", "rep"), axis=0, tiled=False)
    rows = everyone[:, :, :model_width]
    first = model_width + lax.axis_index("ep") * local_experts
    high = lax.dynamic_slice_in_dim(everyone, first, local_experts, axis=2)
    low = lax.dynamic_slice_in_dim(everyone, first + weights.shape[1], local_experts, axis=2)
    local_weights = high.astype(jnp.float32) + low.astype(jnp.float32)
    mask = (local_weights > 0).astype(jnp.float32)
    earlier = (
        jnp.arange(row_count)[:, None] > jnp.arange(row_count)[None, :]
    ).astype(jnp.float32)
    rank = jnp.einsum("ij,sje->sie", earlier, mask)
    slots = jnp.arange(capacity, dtype=jnp.float32)
    placing = jnp.where(
        (rank[:, :, :, None] == slots) & (mask[:, :, :, None] > 0), 1.0, 0.0
    )
    slot_weight = jnp.sum(placing * local_weights[:, :, :, None], axis=1)
    placing = placing.astype(jnp.bfloat16).reshape(sources, row_count, local_experts * capacity)
    grouped = jnp.einsum(
        "sit,sid->std", placing, rows, preferred_element_type=jnp.float32
    ).astype(jnp.bfloat16)
    grouped = grouped.reshape(sources, local_experts, capacity, model_width)
    gate_proj = jnp.einsum(
        "serd,edw->serw", grouped, gate_weight, preferred_element_type=jnp.float32
    )
    up_proj = jnp.einsum("serd,edw->serw", grouped, up_weight, preferred_element_type=jnp.float32)
    active = (jax.nn.silu(gate_proj) * up_proj * slot_weight[..., None]).astype(jnp.bfloat16)
    part = jnp.einsum(
        "serw,edw->serd", active, down_weight, preferred_element_type=jnp.float32
    ).astype(jnp.bfloat16)
    part = part.reshape(sources, local_experts * capacity, model_width)
    share = jnp.einsum("sit,std->sid", placing, part, preferred_element_type=jnp.float32)
    share = share.astype(jnp.bfloat16).reshape(sources * row_count, model_width)
    expert_mix = lax.psum_scatter(share, ("ep", "rep"), scatter_dimension=0, tiled=True)
    total = mixed_stream + expert_mix.astype(jnp.float32)
    return rms_scale(total, final_gain).astype(jnp.bfloat16)


MESH = pl.DeviceIdType.MESH
LINE = 4
OWN, FLIP_X, FLIP_Y, FLIP_BOTH = 0, 1, 2, 3
GO_ACROSS, BACK_ACROSS = 512, 128
COUNTS = (
    ("right", LINE), ("left", LINE), ("x_low", LINE), ("x_high", LINE), ("y_low", LINE),
    ("y_high", LINE), ("far_low", LINE), ("far_high", LINE), ("pass", 4), ("pass_narrow", 1),
    ("plane", 4), ("plane_right", LINE), ("plane_left", LINE),
    ("share", 4), ("y_first", LINE), ("x_first", LINE), ("x_next", LINE), ("y_next", LINE),
    ("x_last", LINE), ("y_last", LINE), ("line_end", LINE), ("back_line", LINE), ("back_plane", 4),
)
BASE = {name: sum(count for _, count in COUNTS[:i]) for i, (name, _) in enumerate(COUNTS)}
STRIDE = sum(count for _, count in COUNTS)
COPIES = 2 * STRIDE + 2


def wave_kernel(
    context_ref, residual_ref, attn_gain_ref, router_ref, ids_ref, gain_ref,
    proj_hbm, gate_hbm, up_hbm, down_hbm, out_ref, block, mixed, rows, gate, up, down, grouped, hits, weighted,
    comb, sib, first, follow, final, line_sum, back_line, back_plane, done, got,
    proj_sem, weight_sem, send_sem, recv_sem,
):
    half = block.shape[0] // 2
    quarter = half // 2
    width = mixed.shape[1]
    extra = block.shape[1] - width
    expert_count = router_ref.shape[0]
    piece = down.shape[2]
    local = gate.shape[0]
    chunk = 2 * LINE * half
    slots = LINE * capacity
    tile = 512

    ep, rep = lax.axis_index("ep"), lax.axis_index("rep")
    z, x, y, core = ep // 2, ep % 2, rep // 2, rep % 2
    across_x = (z * 2 + (1 - x), rep)
    across_y = (ep, (1 - y) * 2 + core)
    diagonal = (z * 2 + (1 - x), (1 - y) * 2 + core)
    sibling = (ep, y * 2 + (1 - core))
    planes = {FLIP_X: across_x, FLIP_Y: across_y, FLIP_BOTH: diagonal}

    def along_z(step):
        return (((z + step) % LINE) * 2 + x, rep)

    peers = [across_x, across_y, diagonal, sibling] + [along_z(step) for step in (1, 2, 3)]
    barrier = pltpu.get_barrier_semaphore()
    for peer in peers:
        pl.semaphore_signal(barrier, inc=1, device_id=peer, device_id_type=MESH)
    weight_copies = [
        pltpu.make_async_copy(source, target, weight_sem.at[i])
        for i, (source, target) in enumerate(((gate_hbm, gate), (up_hbm, up), (down_hbm, down)))
    ]
    proj_copies = [
        pltpu.make_async_copy(
            proj_hbm.at[:, pl.ds(i * piece, piece)], down.at[i], proj_sem.at[i]
        )
        for i in range(width // piece)
    ]
    for copy in proj_copies:
        copy.start()

    slim = pl.ds(0, GO_ACROSS)
    wide = pl.ds(GO_ACROSS, width + extra - GO_ACROSS)
    narrow = pl.ds(0, BACK_ACROSS)
    body = pl.ds(BACK_ACROSS, width - BACK_ACROSS)
    low, high = pl.ds(0, quarter), pl.ds(quarter, quarter)

    def remote(index, source, target, device):
        return pltpu.make_async_remote_copy(
            src_ref=source, dst_ref=target, send_sem=send_sem.at[index],
            recv_sem=recv_sem.at[index], device_id=device, device_id_type=MESH,
        )

    def column(k):
        return (z + k) % LINE

    tours = tuple(
        sum(place * LINE**i for i, place in enumerate(tour))
        for tour in ((0, 1, 2, 3), (1, 0, 2, 3), (2, 3, 1, 0), (3, 2, 1, 0))
    )
    tour = jnp.where(z < 2, jnp.where(z == 0, *tours[:2]), jnp.where(z == 2, *tours[2:]))

    def stop(n):
        power = 1
        for i in range(1, LINE):
            power = power * (1 + (LINE - 1) * jnp.where(n >= i, 1, 0))
        return (tour // power) % LINE

    def copy_of(name, w, k):
        index = w * STRIDE + BASE[name] + k
        if name == "right":
            at = rows.at[w, OWN, (z - k + LINE) % LINE, core, :, wide]
            pair = at, at, along_z(1)
        elif name == "left":
            at = rows.at[w, OWN, (z + k) % LINE, core, :, wide]
            pair = at, at, along_z(LINE - 1)
        elif name == "plane_right":
            at = rows.at[w, :, (z - k + LINE) % LINE, core, :, slim]
            pair = at, at, along_z(1)
        elif name == "plane_left":
            at = rows.at[w, :, (z + k) % LINE, core, :, slim]
            pair = at, at, along_z(LINE - 1)
        elif name in ("x_low", "x_high"):
            part = low if name == "x_low" else high
            pair = (
                rows.at[w, OWN, k, core, part, wide], rows.at[w, FLIP_X, k, core, part, wide],
                across_x,
            )
        elif name in ("y_low", "y_high"):
            part = low if name == "y_low" else high
            pair = (
                rows.at[w, OWN, k, core, part, wide], rows.at[w, FLIP_Y, k, core, part, wide],
                across_y,
            )
        elif name == "far_low":
            pair = (
                rows.at[w, FLIP_X, k, core, low, wide], rows.at[w, FLIP_BOTH, k, core, low, wide],
                across_y,
            )
        elif name == "far_high":
            pair = (
                rows.at[w, FLIP_Y, k, core, high, wide],
                rows.at[w, FLIP_BOTH, k, core, high, wide], across_x,
            )
        elif name == "pass":
            at = rows.at[w, k, :, core, :, wide]
            pair = at, at, sibling
        elif name == "pass_narrow":
            at = rows.at[w, :, :, core, :, slim]
            pair = at, at, sibling
        elif name == "plane":
            pair = rows.at[w, OWN, z, core, :, slim], rows.at[w, k, z, core, :, slim], planes[k]
        elif name == "share":
            pair = comb.at[w, k, 1 - core], sib.at[w, k], sibling
        elif name == "y_first":
            pair = comb.at[w, FLIP_BOTH, core, column(k), low, body], first.at[w, 0, k], across_y
        elif name == "x_first":
            pair = comb.at[w, FLIP_BOTH, core, column(k), high, body], first.at[w, 1, k], across_x
        elif name == "x_next":
            pair = comb.at[w, FLIP_X, core, column(k), high, body], follow.at[w, 1, k], across_x
        elif name == "y_next":
            pair = comb.at[w, FLIP_Y, core, column(k), low, body], follow.at[w, 0, k], across_y
        elif name == "x_last":
            pair = comb.at[w, FLIP_X, core, column(k), low, body], final.at[w, 0, k], across_x
        elif name == "y_last":
            pair = comb.at[w, FLIP_Y, core, column(k), high, body], final.at[w, 1, k], across_y
        elif name == "line_end":
            pair = (
                comb.at[w, OWN, core, column(k), :, body], line_sum.at[w, k - 1], along_z(k)
            )
        elif name == "back_line":
            pair = comb.at[w, :, core, column(k), :, narrow], back_line.at[w, k - 1], along_z(k)
        elif name == "back_plane":
            pair = comb.at[w, k, core, z, :, narrow], back_plane.at[w, k - 1], planes[k]
        return remote(index, *pair)

    def start(name, w, k):
        copy_of(name, w, k).start()

    def arrive(name, w, k):
        copy_of(name, w, k).wait_recv()

    def spread(w, k):
        for name in ("x_low", "y_high", "y_low", "x_high"):
            start(name, w, k)

    def start_line(w, right, left):
        pl.when((z > 0) & (z < LINE // 2))(lambda: start(left, w, 0))
        pl.when(z < LINE - 1)(lambda: start(right, w, 0))
        pl.when(z >= LINE // 2)(lambda: start(left, w, 0))

    def begin(w):
        for k in (FLIP_X, FLIP_Y, FLIP_BOTH):
            start("plane", w, k)
        start_line(w, "right", "left")

    def plane_next(w):
        for k in (FLIP_X, FLIP_Y, FLIP_BOTH):
            arrive("plane", w, k)
        start_line(w, "plane_right", "plane_left")

    def along(w, n, right, left, at):
        source = stop(n)
        index = w * STRIDE + jnp.where(
            source < z, BASE[right] + z - source - 1, BASE[left] + source - z - 1
        )
        remote(index, at(source), at(source), across_x).wait_recv()
        pl.when((source < z) & (z < LINE - 1))(lambda: start(right, w, z - source))
        pl.when((source > z) & (z > 0))(lambda: start(left, w, source - z))
        return source

    def line_next(w, n):
        spread(w, along(w, n, "right", "left", lambda k: rows.at[w, OWN, k, core, :, wide]))

    def narrow_next(w, n):
        along(w, n, "plane_right", "plane_left", lambda k: rows.at[w, :, k, core, :, slim])

    def forward(w, n):
        k = stop(n)
        arrive("x_low", w, k)
        start("far_low", w, k)
        arrive("y_high", w, k)
        start("far_high", w, k)

    def pass_x(w):
        for k in range(LINE):
            arrive("x_high", w, k)
        start("pass", w, FLIP_X)

    def pass_y(w):
        for k in range(LINE):
            arrive("y_low", w, k)
        start("pass", w, FLIP_Y)

    def pass_both(w):
        for k in range(LINE):
            arrive("far_low", w, k)
            arrive("far_high", w, k)
        start("pass", w, FLIP_BOTH)

    column_of = lax.broadcasted_iota(jnp.int32, (16, extra), 1)
    wanted = lax.broadcasted_iota(jnp.int32, (16, extra), 0)
    pick = jnp.where((column_of == ep * local + wanted) & (wanted < local), 1.0, 0.0).astype(
        jnp.bfloat16
    )
    above = lax.broadcasted_iota(jnp.int32, (chunk, chunk), 0)
    below = lax.broadcasted_iota(jnp.int32, (chunk, chunk), 1)
    earlier = jnp.where(
        (above < below) & (above // (2 * half) == below // (2 * half)), 1.0, 0.0
    ).astype(jnp.bfloat16)
    start_slot = (
        (lax.broadcasted_iota(jnp.int32, (16, chunk), 1) // (2 * half)) * capacity
    ).astype(jnp.float32)
    slot_number = lax.broadcasted_iota(jnp.int32, (slots, chunk), 0).astype(jnp.float32)

    def gather(w, place):
        arrive("pass", w, place)
        packed = rows[w, place, :, :, :, width:].reshape(chunk, extra)
        weight = lax.dot_general(
            pick, packed, (((1,), (1,)), ((), ())), preferred_element_type=jnp.float32
        )
        mask = jnp.where(weight > 0, 1.0, 0.0)
        rank = jnp.dot(mask.astype(jnp.bfloat16), earlier, preferred_element_type=jnp.float32)
        target = jnp.where(mask > 0, start_slot + rank, -1.0)
        for e in range(local):
            hit = target[e : e + 1, :] == slot_number
            hits[place, e] = jnp.where(hit, 1.0, 0.0).astype(jnp.bfloat16)
            weighted[place, e] = jnp.where(hit, weight[e : e + 1, :], 0.0).astype(jnp.bfloat16)
        fill(w, place, pl.ds(GO_ACROSS, width - GO_ACROSS))

    def fill(w, place, span):
        found = jnp.dot(
            hits[place].reshape(local * slots, chunk),
            rows[w, place, :, :, :, span].reshape(chunk, span.size),
            preferred_element_type=jnp.float32,
        )
        grouped[:, place * slots : (place + 1) * slots, span] = found.astype(
            jnp.bfloat16
        ).reshape(local, slots, span.size)

    def gather_narrow(w):
        arrive("pass_narrow", w, 0)
        for place in range(4):
            fill(w, place, slim)

    def run_experts(beside):
        @pl.loop(0, local // 2)
        def _(i):
            beside(i)
            active = []
            for e in (2 * i, 2 * i + 1):
                batch = grouped[e]
                gate_proj = jnp.dot(batch, gate[e], preferred_element_type=jnp.float32)
                up_proj = jnp.dot(batch, up[e], preferred_element_type=jnp.float32)
                value = gate_proj / (1.0 + jnp.exp(-gate_proj)) * up_proj
                active.append(value.astype(jnp.bfloat16))
            for e, value in zip((2 * i, 2 * i + 1), active):
                for t in range(width // tile):
                    part = lax.dot_general(
                        value, down[e, t * tile : (t + 1) * tile, :], (((1,), (1,)), ((), ())),
                        preferred_element_type=jnp.float32,
                    )
                    grouped[e, :, t * tile : (t + 1) * tile] = part.astype(jnp.bfloat16)

    def combine(w, place):
        table = weighted[place].reshape(local * slots, chunk)
        piece = grouped[:, place * slots : (place + 1) * slots, :].reshape(local * slots, width)
        result = lax.dot_general(
            table, piece, (((0,), (0,)), ((), ())), preferred_element_type=jnp.float32
        ).astype(jnp.bfloat16).reshape(LINE, 2, half, width)
        for part in range(2):
            comb[w, place, part] = result[:, part]
        start("share", w, place)

    def add_into(target, *terms):
        total = target[...].astype(jnp.float32)
        for term in terms:
            total = total + term[...].astype(jnp.float32)
        target[...] = total.astype(jnp.bfloat16)

    def mine(w, place, k, part, span):
        return comb.at[w, place, core, column(k), part, span]

    def theirs(w, place, k, part, span):
        return sib.at[w, place, column(k), part, span]

    every = pl.ds(0, half)

    def send_both(w):
        arrive("share", w, FLIP_BOTH)
        for k in late:
            add_into(
                mine(w, FLIP_BOTH, k, every, body), theirs(w, FLIP_BOTH, k, every, body)
            )
            start("y_first", w, k)
            start("x_first", w, k)

    def send_narrow(w):
        arrive("share", w, OWN)
        for k in late[:-1]:
            for place in range(4):
                add_into(mine(w, place, k, every, narrow), theirs(w, place, k, every, narrow))
            start("back_line", w, k)

    def turn(w, k):
        arrive("y_first", w, k)
        add_into(
            mine(w, FLIP_X, k, low, body), theirs(w, FLIP_X, k, low, body), first.at[w, 0, k]
        )
        start("x_last", w, k)
        arrive("x_first", w, k)
        add_into(
            mine(w, FLIP_Y, k, high, body), theirs(w, FLIP_Y, k, high, body), first.at[w, 1, k]
        )
        start("y_last", w, k)
        add_into(mine(w, FLIP_X, k, high, body), theirs(w, FLIP_X, k, high, body))
        start("x_next", w, k)
        add_into(mine(w, FLIP_Y, k, low, body), theirs(w, FLIP_Y, k, low, body))
        start("y_next", w, k)

    def turn_narrow(w):
        for k in late[:-1]:
            arrive("back_line", w, k)
        for place in (FLIP_BOTH, FLIP_X, FLIP_Y, OWN):
            add_into(
                mine(w, place, 0, every, narrow), theirs(w, place, 0, every, narrow),
                *(back_line.at[w, k, place] for k in range(LINE - 1)),
            )
            if place != OWN:
                start("back_plane", w, place)

    def finish(w, k):
        arrive("y_next", w, k)
        arrive("x_last", w, k)
        add_into(
            mine(w, OWN, k, low, body), theirs(w, OWN, k, low, body),
            follow.at[w, 0, k], final.at[w, 0, k],
        )
        arrive("x_next", w, k)
        arrive("y_last", w, k)
        add_into(
            mine(w, OWN, k, high, body), theirs(w, OWN, k, high, body),
            follow.at[w, 1, k], final.at[w, 1, k],
        )

    def conclude(w):
        for k in late[:-1]:
            arrive("line_end", w, k)
        for place in (FLIP_X, FLIP_Y, FLIP_BOTH):
            arrive("back_plane", w, place)
        total = comb[w, OWN, core, z, :, body].astype(jnp.float32)
        for k in range(LINE - 1):
            total = total + line_sum[w, k].astype(jnp.float32)
        done[w, :, body] = total
        total = comb[w, OWN, core, z, :, narrow].astype(jnp.float32)
        for k in range(3):
            total = total + back_plane[w, k].astype(jnp.float32)
        done[w, :, narrow] = total

    late = (2, 1, 3, 0)
    skip = ("plane", "line_end", "back_line", "back_plane")
    moves = {"right": -1, "left": 1, "plane_right": -1, "plane_left": 1}
    ends = (
        "y_first", "x_first", "x_next", "y_next", "x_last", "y_last", "line_end", "back_line",
        "back_plane",
    )

    def drain(w, names):
        for name, count in COUNTS:
            if name not in names:
                continue
            for k in range(LINE - 1 if name in moves else count):
                if name in moves:
                    sent = (z > 0) & (z + k < LINE)
                    if moves[name] < 0:
                        sent = (z >= k) & (z < LINE - 1)
                    pl.when(sent)(functools.partial(lambda n, i: copy_of(n, w, i).wait_send(), name, k))
                elif k or name not in skip:
                    copy_of(name, w, k).wait_send()

    square = jnp.zeros((2 * half, 1), jnp.float32)
    for i, copy in enumerate(proj_copies):
        copy.wait()
        if i in (1, 3):
            weight_copies[i // 2].start()
        span = pl.ds(i * piece, piece)
        stream = residual_ref[:, span].astype(jnp.float32) + jnp.dot(
            context_ref[...], down[i], preferred_element_type=jnp.float32
        )
        mixed[:, span] = stream
        square = square + jnp.sum(stream * stream, axis=1, keepdims=True)
    scale = lax.rsqrt(square * (1.0 / width) + epsilon)
    normed = (mixed[...] * scale * attn_gain_ref[...].astype(jnp.float32).reshape(1, width)).astype(jnp.bfloat16)
    block[:, :width] = normed
    logits = lax.dot_general(
        normed, router_ref[...], (((1,), (1,)), ((), ())), preferred_element_type=jnp.float32
    )
    raised = jnp.exp(logits - jnp.max(logits, axis=1, keepdims=True))
    probs = raised / jnp.sum(raised, axis=1, keepdims=True)
    expert = lax.broadcasted_iota(jnp.int32, (expert_count, 2 * half), 0)
    named = ids_ref[0:1, :] == expert
    for i in range(1, ids_ref.shape[0]):
        named = named | (ids_ref[i : i + 1, :] == expert)
    unit = jnp.where(
        lax.broadcasted_iota(jnp.int32, (2 * half, 2 * half), 0)
        == lax.broadcasted_iota(jnp.int32, (2 * half, 2 * half), 1), 1.0, 0.0
    ).astype(jnp.bfloat16)
    chosen = lax.dot_general(
        unit, jnp.where(named, 1.0, 0.0).astype(jnp.bfloat16), (((1,), (1,)), ((), ())),
        preferred_element_type=jnp.float32,
    )
    block[:, width : width + expert_count] = jnp.where(chosen > 0.5, probs, 0.0).astype(
        jnp.bfloat16
    )
    block[:, width + expert_count :] = jnp.zeros((2 * half, extra - expert_count), jnp.bfloat16)
    pl.semaphore_wait(barrier, len(peers))
    rows[core, OWN, z, core] = block[pl.ds(pl.multiple_of(core * half, half), half)]
    given = block.at[pl.ds(pl.multiple_of((1 - core) * half, half), half)]
    taken = rows.at[1 - core, OWN, z, core]
    exchange = remote(2 * STRIDE, given, rows.at[core, OWN, z, 1 - core], sibling)
    exchange.start()
    remote(2 * STRIDE, taken, taken, sibling).wait_recv()

    begin(0)
    spread(0, z)
    line_next(0, 1)
    inner = (z > 0) & (z < LINE - 1)
    pl.when(inner)(lambda: line_next(0, 2))
    plane_next(0)
    forward(0, 0)
    pl.when(~inner)(lambda: line_next(0, 2))
    forward(0, 1)
    line_next(0, 3)
    start("pass", 0, OWN)
    narrow_next(0, 1)
    forward(0, 2)
    narrow_next(0, 2)
    forward(0, 3)
    weight_copies[2].start()
    narrow_next(0, 3)
    begin(1)
    start("pass_narrow", 0, 0)
    gather(0, OWN)
    pass_x(0)
    pass_y(0)
    spread(1, z)
    gather(0, FLIP_X)
    pass_both(0)
    gather(0, FLIP_Y)
    line_next(1, 1)
    gather(0, FLIP_BOTH)
    gather_narrow(0)
    for copy in weight_copies:
        copy.wait()

    def beside_first(i):
        @pl.when(i == 1)
        def _():
            plane_next(1)
            forward(1, 0)

        @pl.when(i >= 2)
        def _():
            line_next(1, i)

        @pl.when(i == 3)
        def _():
            forward(1, 1)

    run_experts(beside_first)
    start("pass", 1, OWN)
    narrow_next(1, 1)
    forward(1, 2)
    combine(0, FLIP_BOTH)
    forward(1, 3)
    narrow_next(1, 2)
    combine(0, FLIP_X)
    send_both(0)
    pass_x(1)
    combine(0, FLIP_Y)
    narrow_next(1, 3)
    arrive("share", 0, FLIP_X)
    combine(0, OWN)
    arrive("share", 0, FLIP_Y)
    turn(0, late[0])
    pass_y(1)
    start("pass_narrow", 1, 0)
    gather(1, OWN)
    turn(0, late[1])
    send_narrow(0)
    gather(1, FLIP_X)
    turn(0, late[2])
    pass_both(1)
    gather(1, FLIP_Y)
    turn(0, late[3])
    gather(1, FLIP_BOTH)
    gather_narrow(1)

    def finish_line(w, k):
        finish(w, k)
        if k:
            start("line_end", w, k)

    def beside_second(i):
        @pl.when(i == 2)
        def _():
            turn_narrow(0)

        @pl.when(i == 3)
        def _():
            finish_line(0, late[0])

    run_experts(beside_second)
    combine(1, FLIP_BOTH)
    finish_line(0, late[1])
    combine(1, FLIP_X)
    finish_line(0, late[2])
    send_both(1)
    combine(1, FLIP_Y)
    finish_line(0, late[3])
    arrive("share", 1, FLIP_X)
    combine(1, OWN)
    arrive("share", 1, FLIP_Y)
    turn(1, late[0])
    turn(1, late[1])
    send_narrow(1)
    turn(1, late[2])
    drain(0, [name for name, _ in COUNTS])
    drain(1, [name for name, _ in COUNTS if name not in ends])
    exchange.wait_send()
    finish_line(1, late[0])
    turn(1, late[3])
    turn_narrow(1)
    conclude(0)
    finish_line(1, late[1])
    finish_line(1, late[2])
    finish_line(1, late[3])
    conclude(1)
    hand_over = remote(2 * STRIDE + 1, done.at[1 - core], got, sibling)
    hand_over.start()
    gain = gain_ref[...].astype(jnp.float32).reshape(1, width)

    def finalize(total, part):
        span = pl.ds(pl.multiple_of(part * half, half), half)
        total = total + mixed[span]
        mean_square = jnp.mean(total * total, axis=-1, keepdims=True)
        out_ref[span] = (total * lax.rsqrt(mean_square + epsilon) * gain).astype(jnp.bfloat16)

    finalize(done[core], core)
    hand_over.wait_recv()
    finalize(got[...], 1 - core)
    hand_over.wait_send()
    drain(1, ends)


def waves(
    context, residual, out_proj, attn_gain, router, expert_ids,
    gate_weight, up_weight, down_weight, final_gain,
):
    row_count, width = context.shape
    padded = width + 2 * router.shape[1]
    half = row_count // 2
    quarter = half // 2
    local = gate_weight.shape[0]
    slots = LINE * capacity
    chunk = 2 * LINE * half
    rest = width - BACK_ACROSS
    low = jnp.bfloat16
    vmem = pl.BlockSpec(memory_space=pltpu.VMEM)
    hbm = pl.BlockSpec(memory_space=pl.ANY)
    return pl.pallas_call(
        wave_kernel,
        out_shape=jax.ShapeDtypeStruct((row_count, width), low),
        in_specs=[vmem] * 6 + [hbm] * 4,
        out_specs=vmem,
        scratch_shapes=[
            pltpu.VMEM((row_count, padded), low),
            pltpu.VMEM((row_count, width), jnp.float32),
            pltpu.VMEM((2, 4, LINE, 2, half, padded), low),
            pltpu.VMEM(gate_weight.shape, low),
            pltpu.VMEM(up_weight.shape, low),
            pltpu.VMEM(down_weight.shape, low),
            pltpu.VMEM((local, 4 * slots, width), low),
            pltpu.VMEM((4, local, slots, chunk), low),
            pltpu.VMEM((4, local, slots, chunk), low),
            pltpu.VMEM((2, 4, 2, LINE, half, width), low),
            pltpu.VMEM((2, 4, LINE, half, width), low),
            pltpu.VMEM((2, 2, LINE, quarter, rest), low),
            pltpu.VMEM((2, 2, LINE, quarter, rest), low),
            pltpu.VMEM((2, 2, LINE, quarter, rest), low),
            pltpu.VMEM((2, LINE - 1, half, rest), low),
            pltpu.VMEM((2, LINE - 1, 4, half, BACK_ACROSS), low),
            pltpu.VMEM((2, 3, half, BACK_ACROSS), low),
            pltpu.VMEM((2, half, width), jnp.float32),
            pltpu.VMEM((half, width), jnp.float32),
            pltpu.SemaphoreType.DMA((width // down_weight.shape[2],)),
            pltpu.SemaphoreType.DMA((3,)),
            pltpu.SemaphoreType.DMA((COPIES,)),
            pltpu.SemaphoreType.DMA((COPIES,)),
        ],
        compiler_params=pltpu.CompilerParams(
            collective_id=0, has_side_effects=True, vmem_limit_bytes=63 * 1024 * 1024
        ),
    )(
        context, residual, attn_gain, router.T, expert_ids.T, final_gain, out_proj,
        gate_weight, up_weight, down_weight,
    )


def solution(mesh):
    per_device = waves if dict(mesh.shape) == {"ep": 2 * LINE, "rep": 4} else gathered
    in_specs = (
        P(("ep", "rep"), None),
        P(("ep", "rep"), None),
        P(),
        P(),
        P(),
        P(("ep", "rep"), None),
        P("ep", None, "rep"),
        P("ep", None, "rep"),
        P("ep", None, "rep"),
        P(),
    )
    out_specs = P(("ep", "rep"), None)
    return jax.shard_map(
        per_device, mesh=mesh, in_specs=in_specs, out_specs=out_specs, check_vma=False
    )
```
